128 devices in a mesh: row: 32 (over z, x, core), col: 4 (over y).
Axes of the slice: x: 4, y: 4, z: 4, core: 2. Of those that a mesh axis runs over, the one named last changes fastest.
Arguments:
- factor_u: float32 [1, 32, 2, 4, 512, 128], P(None, 'row', None, 'col'), may hold values from -6 to 6
- factor_v: float32 [1, 32, 2, 4, 512, 128], P(None, 'row', None, 'col'), may hold values from -6 to 6
- near_field: float32 [2, 512, 512], replicated, as said below
- sketch: float32 [2, 512, 128], replicated, may hold values from -6 to 6
- tile_ranks: int32 [3, 1, 32, 2, 4], P(None, None, None, None, 'col'), may hold values from 1 to 128, as said below
Outputs:
- out_u: float32 [1, 32, 2, 4, 512, 128], P(None, 'row', None, 'col')
- out_v: float32 [1, 32, 2, 4, 512, 128], P(None, 'row', None, 'col')
The draws below stay inside these ranges and needn't reach their ends.
Inputs may be any that keep to these rules, and one draw needn't show every extreme that they name: tile_ranks[0] is at least 16 and equals 128 on every tile (i, i); tile_ranks[1] lies between tile_ranks[0] - tile_ranks[0] // 2 and tile_ranks[0] - max(1, tile_ranks[0] // 4); tile_ranks[2] is at least 1 and at most tile_ranks[1], and when tile_ranks[1] > 1 it is at most tile_ranks[1] - max(1, tile_ranks[1] // 4). The diagonal entries of near_field[0] and near_field[1] lie between 1 and 4.
All inputs are finite; a program needn't handle non-finite values.
Results may differ from the reference program's by a relative error of at most 0.0003.
Values sent between devices are 32-bit elements; how exact they have to be, the bound alone decides.
No kernel may reach another device: no remote copies, remote signals or barrier semaphores. Data moves between devices by JAX's collectives and lax.ppermute only.
A program may use at most 64 MiB of HBM per device.

```python
import math
import jax
import jax.numpy as jnp
from jax import lax

TILE = 512
KMAX = 128
NS_STEPS = 3
TRD = 1
TCD = 2
N_ROW = 32
N_COL = 4


def draw_near_field(key, part):
    key_diagonal, key_spread = jax.random.split(jax.random.fold_in(key, 11))
    identity = jnp.eye(TILE, dtype=jnp.float32)
    diagonal = jnp.exp(jax.random.uniform(key_diagonal, (2, TILE), jnp.float32, 0.0, 1.3862943))
    spread = jax.random.normal(key_spread, (2, TILE, TILE), jnp.float32)
    spread = spread * (0.1 / jnp.sqrt(jnp.float32(TILE)))
    diagonal = jnp.clip(diagonal, 1.0, 4.0)
    return spread * (1.0 - identity) + diagonal[:, :, None] * identity


def draw_tile_ranks(key, part):
    row_count = TRD * N_ROW
    col_count = TCD * N_COL
    label_count = max(row_count, col_count)
    key_list = jax.random.split(jax.random.fold_in(key, 29), 5)
    groups = jax.random.randint(key_list[0], (label_count,), 0, 4)
    heavy_pair = (groups[:row_count, None] == groups[None, :col_count]).astype(jnp.int32)
    base_rank = jax.random.randint(key_list[1], (row_count, col_count), KMAX // 8, KMAX // 2 + 1)
    extra_rank = jax.random.randint(key_list[2], (row_count, col_count), 0, KMAX // 2 + 1) * heavy_pair
    rank_first = jnp.minimum(base_rank + extra_rank, KMAX)
    on_diagonal = jnp.arange(row_count)[:, None] == jnp.arange(col_count)[None, :]
    rank_first = jnp.where(on_diagonal, KMAX, rank_first)
    low_first = jnp.maximum(1, rank_first // 4)
    rank_second = rank_first - jax.random.randint(key_list[3], (row_count, col_count), low_first, rank_first // 2 + 1)
    low_second = jnp.maximum(1, rank_second // 4)
    high_second = jnp.maximum(low_second, rank_second // 2)
    rank_third = jnp.maximum(1, rank_second - jax.random.randint(key_list[4], (row_count, col_count), low_second, high_second + 1))
    stacked = jnp.stack([rank_first, rank_second, rank_third]).astype(jnp.int32)
    return stacked.reshape(3, TRD, N_ROW, TCD, N_COL)


def steps_of(stream_key, shape, pieces, low, top_value):
    def one(position, blocks):
        steps = jax.random.uniform(jax.random.fold_in(jax.random.fold_in(stream_key, 6), position), (blocks,), jnp.float32, low / len(pieces), top_value / len(pieces))
        return jnp.repeat(jnp.exp(steps), shape[position] // blocks).reshape((-1,) + (1,) * (len(shape) - position - 1))

    factor_of = one(*pieces[0])
    for cut in pieces[1:]:
        factor_of = factor_of * one(*cut)
    return factor_of


def normal_values(stream_key, extent, scale, bound, cuts=(), kind=jnp.bfloat16):
    gain = steps_of(stream_key, extent, cuts, -0.22, 0.18) if cuts else 1.0
    drawn = jax.random.normal(stream_key, extent, jnp.float32) * scale * gain
    return jnp.minimum(jnp.maximum(drawn, -bound), bound).astype(kind)


def setup_inputs(seed: int = 0) -> dict:
    splits = jax.random.split(jax.random.key(seed), 6)
    factor_u = normal_values(splits[0], (TRD, N_ROW, TCD, N_COL, TILE, KMAX), 1.0, 6.0, ((1, 32), (3, 4)), jnp.float32)
    factor_v = normal_values(splits[1], (TRD, N_ROW, TCD, N_COL, TILE, KMAX), 1.0, 6.0, ((1, 32), (3, 4)), jnp.float32)
    near_field = draw_near_field(jax.random.fold_in(splits[5], 71), 0)
    sketch = normal_values(splits[3], (2, TILE, KMAX), 1.0, 6.0, (), jnp.float32)
    tile_ranks = draw_tile_ranks(jax.random.fold_in(splits[5], 71), 0)
    return {"factor_u": factor_u, "factor_v": factor_v, "near_field": near_field, "sketch": sketch, "tile_ranks": tile_ranks}


highest = lax.Precision.HIGHEST

def rank_keep(ranks, width):
    return jnp.arange(width, dtype=jnp.int32) < ranks[..., None]

def orthonormal(basis, keeper):
    gram = jnp.einsum('...tk,...tl->...kl', basis, basis, precision=highest)
    unused = 1.0 - keeper.astype(basis.dtype)
    gram = gram + jnp.eye(basis.shape[-1], dtype=basis.dtype) * unused[..., None, :]
    factor = jnp.linalg.cholesky(gram)
    solved = jax.scipy.linalg.solve_triangular(factor, jnp.swapaxes(basis, -1, -2), lower=True)
    return jnp.swapaxes(solved, -1, -2)

def recompress(full_u, full_v, sketch_block, ranks):
    root_order = math.sqrt(full_u.shape[-2])
    keeper = rank_keep(ranks, sketch_block.shape[-1])
    projected = jnp.einsum('...tq,tk->...qk', full_v, sketch_block, precision=highest)
    basis = jnp.einsum('...tq,...qk->...tk', full_u, projected, precision=highest)
    basis = basis * keeper[..., None, :].astype(basis.dtype)
    ortho = orthonormal(orthonormal(basis, keeper), keeper)
    backward = jnp.einsum('...tq,...tk->...qk', full_u, ortho, precision=highest)
    new_v = jnp.einsum('...tq,...qk->...tk', full_v, backward, precision=highest) / root_order
    return (ortho * root_order, new_v)

def update_tiles(cur_u, cur_v, low_u, low_v, up_u, up_v, sketch_block, ranks):
    far_weight = 1.0 / (8.0 * cur_u.shape[-2])
    core_block = far_weight * jnp.einsum('...tk,...tl->...kl', low_v, up_u, precision=highest)
    product_u = jnp.einsum('...tk,...kl->...tl', low_u, core_block, precision=highest)
    product_u = jnp.broadcast_to(product_u, cur_u.shape)
    full_u = jnp.concatenate([cur_u, -product_u], axis=-1)
    full_v = jnp.concatenate([cur_v, jnp.broadcast_to(up_v, cur_v.shape)], axis=-1)
    return (product_u, recompress(full_u, full_v, sketch_block, ranks))

def newton_inverse(pivot, start_inverse):
    inverse = jnp.diag(start_inverse)
    twice = 2.0 * jnp.eye(pivot.shape[0], dtype=pivot.dtype)
    for newton_step in range(NS_STEPS):
        inverse = jnp.dot(inverse, twice - jnp.dot(pivot, inverse, precision=highest), precision=highest)
    return inverse

def reference(factor_u, factor_v, near_field, sketch, tile_ranks):
    row_count = TRD * N_ROW
    col_count = TCD * N_COL
    cur_u = factor_u.reshape(row_count, col_count, TILE, KMAX)
    cur_v = factor_v.reshape(row_count, col_count, TILE, KMAX)
    all_ranks = tile_ranks.reshape(3, row_count, col_count)
    keeper = rank_keep(all_ranks[0], KMAX).astype(cur_u.dtype)[..., None, :]
    cur_u = cur_u * keeper
    cur_v = cur_v * keeper
    far_weight = 1.0 / (8.0 * TILE)
    tile_row = jnp.arange(row_count, dtype=jnp.int32)[:, None]
    tile_col = jnp.arange(col_count, dtype=jnp.int32)[None, :]
    pivot = near_field[0] + far_weight * jnp.dot(cur_u[0, 0], cur_v[0, 0].T, precision=highest)
    for panel in range(2):
        inverse = newton_inverse(pivot, 1.0 / jnp.diagonal(near_field[panel]))
        low_v = jnp.einsum('st,isk->itk', inverse, cur_v[:, panel], precision=highest)
        up_u = cur_u[panel]
        up_v = cur_v[panel]
        sketch_block = sketch[panel]

        def one_row(items):
            row_u, row_v, lead_u, lead_v, row_ranks = items
            unused_product, fresh_pair = update_tiles(row_u, row_v, lead_u[None], lead_v[None], up_u, up_v, sketch_block, row_ranks)
            return fresh_pair
        fresh_u, fresh_v = lax.map(one_row, (cur_u[panel + 1:], cur_v[panel + 1:], cur_u[panel + 1:, panel], low_v[panel + 1:], all_ranks[panel + 1, panel + 1:]))
        if panel == 0:
            core_block = far_weight * jnp.dot(low_v[1].T, cur_u[0, 1], precision=highest)
            product_one = jnp.dot(cur_u[1, 0], core_block, precision=highest)
            pivot = near_field[1] + far_weight * (jnp.dot(cur_u[1, 1], cur_v[1, 1].T, precision=highest) - jnp.dot(product_one, cur_v[0, 1].T, precision=highest))
        chosen = (tile_row > panel) & (tile_col > panel)
        if panel == 0:
            chosen = chosen & jnp.logical_not((tile_row == 1) & (tile_col == 1))
        chosen = chosen[panel + 1:, :, None, None]
        cur_u = cur_u.at[panel + 1:].set(jnp.where(chosen, fresh_u, cur_u[panel + 1:]))
        cur_v = cur_v.at[panel + 1:].set(jnp.where(chosen, fresh_v, cur_v[panel + 1:]))
        lower_here = tile_row[:, 0] > panel
        cur_v = cur_v.at[:, panel].set(jnp.where(lower_here[:, None, None], low_v, cur_v[:, panel]))
        cur_u = cur_u.at[panel, panel].set(jnp.zeros((TILE, KMAX), cur_u.dtype))
        cur_v = cur_v.at[panel, panel].set(jnp.zeros((TILE, KMAX), cur_v.dtype))
    shape_out = (TRD, N_ROW, TCD, N_COL, TILE, KMAX)
    return (cur_u.reshape(shape_out), cur_v.reshape(shape_out))
```

```python
import functools
import math
import jax
import jax.numpy as jnp
from jax import lax
from jax.experimental import pallas as pl
from jax.experimental.pallas import tpu as pltpu
from jax.sharding import PartitionSpec as P

F32 = jnp.float32
BF16 = jnp.bfloat16
NN = (((1,), (0,)), ((), ()))
NT = (((1,), (1,)), ((), ()))
TN = (((0,), (0,)), ((), ()))


def dot6(a, b, dims=NN):
    return lax.dot_general(a, b, dims, precision=lax.Precision.HIGHEST, preferred_element_type=F32)


def split(a):
    high = a.astype(BF16)
    return high, (a - high.astype(F32)).astype(BF16)


def dot1(a, b, dims=NN):
    return lax.dot_general(a, b, dims, preferred_element_type=F32)


def dot3(a, b, dims=NN):
    ah, al = a if isinstance(a, tuple) else split(a)
    bh, bl = b if isinstance(b, tuple) else split(b)
    return dot1(ah, bh, dims) + (dot1(ah, bl, dims) + dot1(al, bh, dims))


def iota(shape, axis):
    return lax.broadcasted_iota(jnp.int32, shape, axis)


def eliminate(grams, order):
    count = len(grams)
    lane8 = iota((8, 128), 1)
    row8 = iota((8, 128), 0)
    blocks = [[g[8 * b:8 * b + 8, :] for b in range(order // 8)] for g in grams]
    done = [[] for _ in grams]
    for step in range(order // 8):
        base = 8 * step
        panels, pivots_all = [], []
        for g in range(count):
            panel = blocks[g][step]
            cols = [jnp.broadcast_to(panel[:, base + c:base + c + 1], (8, 128)) for c in range(8)]
            inside = (lane8 >= base) & (lane8 < base + 8)
            work = jnp.where(inside, (lane8 - base == row8).astype(F32), panel)
            scale = jnp.zeros((8, 128), F32)
            for c in range(8):
                pivot = jnp.broadcast_to(cols[c][c:c + 1, :], (8, 128))
                inverse = 1.0 / pivot
                scale = jnp.where(row8 == c, inverse, scale)
                if c < 7:
                    factor = jnp.where(row8 > c, cols[c] * inverse, 0.0)
                    for d in range(c + 1, 8):
                        cols[d] = cols[d] - factor * jnp.broadcast_to(cols[d][c:c + 1, :], (8, 128))
                    work = work - factor * jnp.broadcast_to(work[c:c + 1, :], (8, 128))
            panels.append(work)
            pivots_all.append(scale)
        for g in range(count):
            work, scale = panels[g], pivots_all[g]
            done[g].append(work * jnp.sqrt(scale))
            if step + 1 < order // 8:
                update = dot6(work, work * scale, TN)
                inside = (lane8 >= base) & (lane8 < base + 8)
                for b in range(step + 1, order // 8):
                    blocks[g][b] = jnp.where(inside, 0.0, blocks[g][b]) - update[8 * b:8 * b + 8, :]
    outs = []
    for g in range(count):
        full = jnp.concatenate(done[g], axis=0)
        keep = iota((order, 128), 1) <= iota((order, 128), 0)
        outs.append(jnp.where(keep, full, 0.0))
    return outs


def panel_kernel(order, first, flags, cu, cv, lu, lowt, upu, upv, st, nu, nv, wide_out, ortho, factor):
    tile = cu.shape[1]
    width = cu.shape[2]
    weight = 1.0 / (8.0 * tile)
    root = math.sqrt(tile)
    lanes = iota((tile, width), 1)
    spare = jnp.zeros((width - order, tile), F32)
    row_g = iota((order, width), 0)
    lane_g = iota((order, width), 1)
    eye = (row_g == lane_g).astype(F32)
    full_us, full_vs, bases, grams, units = [], [], [], [], []
    low = split(lowt[...])
    lead = split(lu[...])
    sketch = st[...]
    for s in range(2):
        own_u = cu[s]
        up_u = upu[s]
        if first:
            own_u = jnp.where(lanes < flags[2 + s], own_u, 0.0)
            up_u = jnp.where(lanes < flags[4 + s], up_u, 0.0)
        core = weight * dot3(low, up_u)
        wide = dot3(lead, core)
        if s == 0 and first:
            wide_out[...] = wide
        full_u = jnp.concatenate([own_u, -wide], axis=1)
        full_v = jnp.concatenate([cv[s], upv[s]], axis=1)
        projected = dot6(sketch, full_v)
        basis = dot6(projected, full_u, NT)
        basis = jnp.where(iota((order, tile), 0) < flags[s], basis, 0.0)
        basis = jnp.concatenate([basis, spare], axis=0)
        unit = jnp.where((row_g == lane_g) & (row_g >= flags[s]), 1.0, 0.0)
        grams.append(dot6(basis[:order], basis, NT) + unit)
        full_us.append(full_u)
        full_vs.append(full_v)
        bases.append(basis)
        units.append(unit)
    inverses = eliminate(grams, order)
    twice, defect = [], jnp.zeros((), F32)
    for s in range(2):
        once = dot6(inverses[s], bases[s])
        ortho[s, :order] = once
        ortho[s, order:] = spare
        gram = dot6(once, jnp.concatenate([once, spare], axis=0), NT) + units[s]
        factor[s] = gram
        off = gram - eye
        defect = jnp.maximum(defect, jnp.sum(off * off))
    near = defect < 1e-6

    @pl.when(near)
    def _():
        for s in range(2):
            off = factor[s] - eye
            half = jnp.where(lane_g < row_g, off, jnp.where(lane_g == row_g, 0.5 * off, 0.0))
            once = ortho[s]
            ortho[s, :order] = once[:order] - dot1(half.astype(BF16), once.astype(BF16))

    @pl.when(jnp.logical_not(near))
    def _():
        again = eliminate([factor[0], factor[1]], order)
        for s in range(2):
            ortho[s, :order] = dot6(again[s], ortho[s])

    for s in range(2):
        basis = ortho[s]
        back = dot3(basis, full_us[s])
        fresh_v = dot3(full_vs[s], back, NT) * (1.0 / root)
        fresh_u = basis.T * root
        keep_u = cu[s]
        keep_v = cv[s]
        if first:
            keep_u = jnp.where(lanes < flags[2 + s], keep_u, 0.0)
            keep_v = jnp.where(lanes < flags[2 + s], keep_v, 0.0)
        if s == 0:
            keep_v = jnp.where(flags[8] == 1, lowt[...].T, keep_v)
            keep_u = jnp.where(flags[9] == 1, 0.0, keep_u)
            keep_v = jnp.where(flags[9] == 1, 0.0, keep_v)
        chosen = flags[6 + s] == 1
        nu[s] = jnp.where(chosen, fresh_u, keep_u)
        nv[s] = jnp.where(chosen, fresh_v, keep_v)


def panel_update(first, flags, cu, cv, lu, lowt, upu, upv, st):
    order = st.shape[0]
    tile, width = lu.shape
    vmem = pl.BlockSpec(memory_space=pltpu.VMEM)
    pair = jax.ShapeDtypeStruct((2, tile, width), F32)
    return pl.pallas_call(
        functools.partial(panel_kernel, order, first),
        out_shape=(pair, pair, jax.ShapeDtypeStruct((tile, width), F32)),
        in_specs=[pl.BlockSpec(memory_space=pltpu.SMEM)] + [vmem] * 7,
        out_specs=(vmem, vmem, vmem),
        scratch_shapes=[pltpu.VMEM((2, width, tile), F32), pltpu.VMEM((2, order, width), F32)],
        compiler_params=pltpu.CompilerParams(vmem_limit_bytes=40 * 1024 * 1024),
    )(flags, cu, cv, lu, lowt, upu, upv, st)


def lower_kernel(pairs, near, *refs):
    us, vs, own_v, rank, out = refs[:pairs], refs[pairs:2 * pairs], refs[2 * pairs], refs[2 * pairs + 1], refs[2 * pairs + 2]
    tile, width = own_v.shape
    weight = 1.0 / (8.0 * tile)
    eye = iota((tile, tile), 0) == iota((tile, tile), 1)
    far = near[...]
    start = 1.0 / jnp.sum(jnp.where(eye, far, 0.0), axis=0, keepdims=True)
    low_rank = dot3(us[0][...], vs[0][...], NT)
    if pairs == 2:
        low_rank = low_rank - dot3(us[1][...], vs[1][...], NT)
    pivot = far + weight * low_rank
    rest = jnp.where(eye, 1.0, 0.0) - pivot * start
    values = jnp.where(iota((tile, width), 1) < rank[0], own_v[...], 0.0).T * start
    parts = split(rest)
    square = dot3(parts, parts)
    values = values + dot3(values, parts)
    parts = split(square)
    fourth = dot3(parts, parts)
    values = values + dot3(values, parts)
    out[...] = values + dot3(values, fourth)


def lower_values(near, us, vs, own_v, rank):
    tile, width = own_v.shape
    vmem = pl.BlockSpec(memory_space=pltpu.VMEM)
    pairs = len(us)
    return pl.pallas_call(
        functools.partial(lower_kernel, pairs),
        out_shape=jax.ShapeDtypeStruct((width, tile), F32),
        in_specs=[vmem] * (2 + 2 * pairs) + [pl.BlockSpec(memory_space=pltpu.SMEM)],
        out_specs=vmem,
        compiler_params=pltpu.CompilerParams(vmem_limit_bytes=40 * 1024 * 1024),
    )(near, *us, *vs, own_v, rank)


Z_COUNT = 4
X_COUNT = 4


def row_of(z, x, core):
    return (z * X_COUNT + x) * 2 + core


def fan_out(value, axis, pair_sets):
    total = None
    for pairs in pair_sets:
        moved = lax.ppermute(value, axis, pairs)
        total = moved if total is None else total + moved
    return total


def share_column(halves, root):
    row = lax.axis_index("row")
    core = row % 2
    x = (row // 2) % X_COUNT
    z = row // (2 * X_COUNT)
    crossed = lax.ppermute(halves[1 - root], "row", [(root, 1 - root)])
    mine = jnp.where(row == root, halves[root], crossed)
    first = fan_out(
        mine,
        "row",
        [[(row_of(0, 0, 0), row_of(k, 0, 0)), (row_of(0, 0, 1), row_of(0, k, 1))] for k in (1, 3, 2)],
    )
    held = jnp.where(row < 2, mine, first)
    second = fan_out(
        held,
        "row",
        [
            [(row_of(z, 0, 0), row_of(z, k, 0)) for z in range(Z_COUNT)]
            + [(row_of(0, x, 1), row_of(k, x, 1)) for x in range(X_COUNT)]
            for k in (1, 3, 2)
        ],
    )
    holder = jnp.where(core == 0, x, z) == 0
    final = jnp.where(holder, held, second)
    other = lax.ppermute(final, "row", [(r, r ^ 1) for r in range(2 * X_COUNT * Z_COUNT)])
    return jnp.where(core == 0, final, other), jnp.where(core == 0, other, final)


def share_row(value, root):
    col = lax.axis_index("col")
    right, left, far = (root + 1) % 4, (root + 3) % 4, (root + 2) % 4
    middle = value.shape[0] // 2
    head, tail = value[:middle], value[middle:]
    head_right = lax.ppermute(head, "col", [(root, right)])
    tail_left = lax.ppermute(tail, "col", [(root, left)])
    via_right = lax.ppermute(jnp.where(col == root, tail, head_right), "col", [(root, right), (right, far)])
    via_left = lax.ppermute(jnp.where(col == root, head, tail_left), "col", [(root, left), (left, far)])
    got_head = jnp.where(col == right, head_right, jnp.where(col == far, via_right, via_left))
    got_tail = jnp.where(col == left, tail_left, jnp.where(col == far, via_left, via_right))
    return jnp.where(col == root, value, jnp.concatenate([got_head, got_tail]))


def body(factor_u, factor_v, near_field, sketch, tile_ranks):
    tile, width = factor_u.shape[4:]
    row = lax.axis_index("row")
    col = lax.axis_index("col")
    own_u = factor_u.reshape(2, tile, width)
    own_v = factor_v.reshape(2, tile, width)
    ranks = tile_ranks.reshape(3, -1, 2)
    own_ranks = lax.dynamic_slice_in_dim(ranks, row, 1, 1)[:, 0]
    order = (width - width // 4, width - width // 4 - (width - width // 4) // 4)
    sketch_t = [sketch[k, :, : order[k]].T for k in range(2)]

    def flags_of(panel):
        slots = jnp.arange(2) * 4 + col
        chosen = (row > panel) & (slots > panel)
        if panel == 0:
            chosen = chosen & jnp.logical_not((row == 1) & (slots == 1))
        lower = (row > panel) & (col == panel)
        pivot = (row == panel) & (col == panel)
        parts = [own_ranks[panel + 1], own_ranks[0], ranks[0, 0], chosen, lower[None], pivot[None]]
        return jnp.concatenate([part.astype(jnp.int32) for part in parts])

    with jax.named_scope("first_share"):
        up_a = share_column((own_u[0], own_v[0]), 0)
        up_b = share_column((own_u[1], own_v[1]), 0)
        lead = share_row(own_u[0], 0)
    with jax.named_scope("first_lower"):
        low = lower_values(near_field[0], [up_a[0]], [up_a[1]], own_v[0], own_ranks[0, :1])
        low = share_row(low, 0)
    with jax.named_scope("pivot_share"):
        corner = share_column((own_u[0], own_v[0]), 1)
    with jax.named_scope("first_update"):
        up_u, up_v = jnp.stack([up_a[0], up_b[0]]), jnp.stack([up_a[1], up_b[1]])
        cur_u, cur_v, wide = panel_update(True, flags_of(0), own_u, own_v, lead, low, up_u, up_v, sketch_t[0])
    with jax.named_scope("second_share"):
        half = tile // 2
        wide = jnp.concatenate(share_column((wide[:half], wide[half:]), 1))
        lead = share_row(cur_u[0], 1)
        fresh = jnp.concatenate([cur_u, cur_v], axis=1)
        fresh_a, fresh_b = share_column((fresh[0], fresh[1]), 1)
    with jax.named_scope("second_lower"):
        full = jnp.full((1,), width, jnp.int32)
        low = lower_values(near_field[1], [corner[0], wide], [corner[1], up_a[1]], cur_v[0], full)
        low = share_row(low, 1)
    with jax.named_scope("second_update"):
        up_u = jnp.stack([fresh_a[:tile], fresh_b[:tile]])
        up_v = jnp.stack([fresh_a[tile:], fresh_b[tile:]])
        cur_u, cur_v, _ = panel_update(False, flags_of(1), cur_u, cur_v, lead, low, up_u, up_v, sketch_t[1])
    shape_out = factor_u.shape
    return cur_u.reshape(shape_out), cur_v.reshape(shape_out)


def solution(mesh):
    tiles = P(None, "row", None, "col", None, None)
    return jax.shard_map(
        body,
        mesh=mesh,
        in_specs=(tiles, tiles, P(), P(), P(None, None, None, None, "col")),
        out_specs=(tiles, tiles),
        check_vma=False,
    )
```

```python
import functools
import math
import jax
import jax.numpy as jnp
from jax import lax
from jax.experimental import pallas as pl
from jax.experimental.pallas import tpu as pltpu
from jax.sharding import PartitionSpec as P

F32 = jnp.float32
BF16 = jnp.bfloat16
NN = (((1,), (0,)), ((), ()))
NT = (((1,), (1,)), ((), ()))
TN = (((0,), (0,)), ((), ()))


def dot6(a, b, dims=NN):
    return lax.dot_general(a, b, dims, precision=lax.Precision.HIGHEST, preferred_element_type=F32)


def split(a):
    high = a.astype(BF16)
    return high, (a - high.astype(F32)).astype(BF16)


def dot1(a, b, dims=NN):
    return lax.dot_general(a, b, dims, preferred_element_type=F32)


def dot3(a, b, dims=NN):
    ah, al = a if isinstance(a, tuple) else split(a)
    bh, bl = b if isinstance(b, tuple) else split(b)
    return dot1(ah, bh, dims) + (dot1(ah, bl, dims) + dot1(al, bh, dims))


def iota(shape, axis):
    return lax.broadcasted_iota(jnp.int32, shape, axis)


def eliminate(grams, order):
    count = len(grams)
    lane8 = iota((8, 128), 1)
    row8 = iota((8, 128), 0)
    blocks = [[g[8 * b:8 * b + 8, :] for b in range(order // 8)] for g in grams]
    done = [[] for _ in grams]
    for step in range(order // 8):
        base = 8 * step
        panels, pivots_all = [], []
        for g in range(count):
            panel = blocks[g][step]
            cols = [jnp.broadcast_to(panel[:, base + c:base + c + 1], (8, 128)) for c in range(8)]
            inside = (lane8 >= base) & (lane8 < base + 8)
            work = jnp.where(inside, (lane8 - base == row8).astype(F32), panel)
            scale = jnp.zeros((8, 128), F32)
            for c in range(8):
                pivot = jnp.broadcast_to(cols[c][c:c + 1, :], (8, 128))
                inverse = 1.0 / pivot
                scale = jnp.where(row8 == c, inverse, scale)
                if c < 7:
                    factor = jnp.where(row8 > c, cols[c] * inverse, 0.0)
                    for d in range(c + 1, 8):
                        cols[d] = cols[d] - factor * jnp.broadcast_to(cols[d][c:c + 1, :], (8, 128))
                    work = work - factor * jnp.broadcast_to(work[c:c + 1, :], (8, 128))
            panels.append(work)
            pivots_all.append(scale)
        for g in range(count):
            work, scale = panels[g], pivots_all[g]
            done[g].append(work * jnp.sqrt(scale))
            if step + 1 < order // 8:
                update = dot6(work, work * scale, TN)
                inside = (lane8 >= base) & (lane8 < base + 8)
                for b in range(step + 1, order // 8):
                    blocks[g][b] = jnp.where(inside, 0.0, blocks[g][b]) - update[8 * b:8 * b + 8, :]
    outs = []
    for g in range(count):
        full = jnp.concatenate(done[g], axis=0)
        keep = iota((order, 128), 1) <= iota((order, 128), 0)
        outs.append(jnp.where(keep, full, 0.0))
    return outs


def wide_of(lead, up):
    weight = 1.0 / (8.0 * lead.shape[1])
    core = weight * dot3(lead[1], up, TN)
    return dot3(lead[0], core)


def series(pivot, start):
    eye = iota(pivot.shape, 0) == iota(pivot.shape, 1)
    rest = split(jnp.where(eye, 1.0, 0.0) - pivot * start)
    square = split(dot3(rest, rest))
    return rest, square, split(dot3(square, square))


def start_of(far, axis):
    eye = iota(far.shape, 0) == iota(far.shape, 1)
    return 1.0 / jnp.sum(jnp.where(eye, far, 0.0), axis=axis, keepdims=True)


def upper_kernel(panel, flags, near, *refs):
    if panel == 0:
        corner, own, out_a, out_b = refs
    else:
        corner, extra, own, out = refs
    tile, width = own.shape[1:]
    weight = 1.0 / (8.0 * tile)
    far = near[panel]
    low_rank = dot3(corner[0], corner[1], NT)
    if panel == 1:
        low_rank = low_rank - dot3(extra[0], extra[1], NT)
    parts = series(far + weight * low_rank, start_of(far, 0))
    lanes = iota((tile, width), 1)
    values = [own[s] for s in range(2)]
    if panel == 0:
        values = [jnp.where(lanes < flags[2 + s], values[s], 0.0) for s in range(2)]
    values = jnp.concatenate(values, axis=1)
    for part in parts[::-1]:
        values = values + dot3(part, values)
    values = values * start_of(far, 1)
    spare = corner[0] if panel == 0 else extra[0]
    first = jnp.where(flags[10] == panel, spare, values[:, :width])
    if panel == 0:
        out_a[...] = first
        out_b[...] = values[:, width:]
    else:
        out[0] = first
        out[1] = values[:, width:]


def lower_kernel(flags, near, up_a, up_b, ours, theirs, fresh_a, fresh_b, own_v, out):
    tile, width = own_v.shape[1:]
    weight = 1.0 / (8.0 * tile)
    left = flags[10] == 0
    even = flags[11] == 0
    far = jnp.where(left, near[0], near[1])
    up_u = jnp.where(even, up_a[...], up_b[...])
    up_v = jnp.where(even, ours[0], theirs[0])
    corner_u = jnp.where(even, theirs[0], ours[0])
    corner_v = jnp.where(even, theirs[1], ours[1])
    wide = jnp.where(even, fresh_a[0], fresh_b[0])
    one_u = jnp.where(left, up_u, corner_u)
    one_v = jnp.where(left, up_v, corner_v)
    two_u = jnp.where(left, 0.0, wide)
    start = start_of(far, 0)
    low_rank = dot3(one_u, one_v, NT) - dot3(two_u, up_v, NT)
    values = own_v[0].T * start
    for part in series(far + weight * low_rank, start):
        values = values + dot3(values, part)
    out[...] = values


def wide_kernel(flags, lead, up_a, up_b, ours, theirs, wide, pack):
    even = flags[11] == 0
    near_up = jnp.where(even, up_a[...], up_b[...])
    far_up = jnp.where(even, up_b[...], up_a[...])
    first = wide_of(lead, near_up)
    wide[0] = first
    wide[1] = wide_of(lead, far_up)
    pack[0] = first
    pack[1] = jnp.where(even, ours[0], theirs[0])


def panel_kernel(order, first, flags, cu, cv, *refs):
    if first:
        wide, ours, theirs, st, nu, nv, pack, ortho, factor = refs
    else:
        lead, ours, theirs, lowt, st, nu, nv, ortho, factor = refs
    tile, width = cu.shape[1:]
    root = math.sqrt(tile)
    lanes = iota((tile, width), 1)
    spare = jnp.zeros((width - order, tile), F32)
    row_g = iota((order, width), 0)
    lane_g = iota((order, width), 1)
    eye = (row_g == lane_g).astype(F32)
    even = flags[11] == 0
    full_us, full_vs, bases, grams, units = [], [], [], [], []
    sketch = st[...]
    for s in range(2):
        own_u = cu[s]
        if first:
            own_u = jnp.where(lanes < flags[2 + s], own_u, 0.0)
            side = wide[s]
            up_v = jnp.where(even, ours[s], theirs[s])
        else:
            side = wide_of(lead, jnp.where(even, ours[s], theirs[s]))
            up_v = jnp.where(even, theirs[s], ours[s])
        full_u = jnp.concatenate([own_u, -side], axis=1)
        full_v = jnp.concatenate([cv[s], up_v], axis=1)
        projected = dot6(sketch, full_v)
        basis = dot6(projected, full_u, NT)
        basis = jnp.where(iota((order, tile), 0) < flags[s], basis, 0.0)
        basis = jnp.concatenate([basis, spare], axis=0)
        unit = jnp.where((row_g == lane_g) & (row_g >= flags[s]), 1.0, 0.0)
        grams.append(dot6(basis[:order], basis, NT) + unit)
        full_us.append(full_u)
        full_vs.append(full_v)
        bases.append(basis)
        units.append(unit)
    inverses = eliminate(grams, order)
    defect = jnp.zeros((), F32)
    for s in range(2):
        once = dot6(inverses[s], bases[s])
        ortho[s, :order] = once
        ortho[s, order:] = spare
        gram = dot6(once, jnp.concatenate([once, spare], axis=0), NT) + units[s]
        factor[s] = gram
        off = gram - eye
        defect = defect + jnp.where(flags[6 + s] == 1, jnp.sum(off * off), 0.0)
    near = defect < 1e-6

    @pl.when(near)
    def _():
        for s in range(2):
            off = factor[s] - eye
            half = jnp.where(lane_g < row_g, off, jnp.where(lane_g == row_g, 0.5 * off, 0.0))
            once = ortho[s]
            ortho[s, :order] = once[:order] - dot1(half.astype(BF16), once.astype(BF16))

    @pl.when(jnp.logical_not(near))
    def _():
        again = eliminate([factor[0], factor[1]], order)
        for s in range(2):
            ortho[s, :order] = dot6(again[s], ortho[s])

    for s in range(2):
        basis = ortho[s]
        back = dot3(basis, full_us[s])
        fresh_v = dot3(full_vs[s], back, NT) * (1.0 / root)
        fresh_u = basis.T * root
        keep_u = cu[s]
        keep_v = cv[s]
        if first:
            keep_u = jnp.where(lanes < flags[2 + s], keep_u, 0.0)
            keep_v = jnp.where(lanes < flags[2 + s], keep_v, 0.0)
        elif s == 0:
            keep_v = jnp.where(flags[8] == 1, lowt[...].T, keep_v)
            keep_u = jnp.where(flags[9] == 1, 0.0, keep_u)
            keep_v = jnp.where(flags[9] == 1, 0.0, keep_v)
        chosen = flags[6 + s] == 1
        new_u = jnp.where(chosen, fresh_u, keep_u)
        new_v = jnp.where(chosen, fresh_v, keep_v)
        nu[s] = new_u
        nv[s] = new_v
        if first and s == 0:
            pack[0] = new_u
            pack[1] = new_v


def call(kernel, shapes, flags, *values, scratch=()):
    vmem = pl.BlockSpec(memory_space=pltpu.VMEM)
    shapes = tuple(jax.ShapeDtypeStruct(shape, F32) for shape in shapes)
    out = pl.pallas_call(
        kernel,
        out_shape=shapes,
        in_specs=[pl.BlockSpec(memory_space=pltpu.SMEM)] + [vmem] * len(values),
        out_specs=(vmem,) * len(shapes),
        scratch_shapes=list(scratch),
        compiler_params=pltpu.CompilerParams(vmem_limit_bytes=40 * 1024 * 1024),
    )(flags, *values)
    return out if len(out) > 1 else out[0]


Z_COUNT = 4
X_COUNT = 4
COLS = 4


def row_of(z, x, core):
    return (z * X_COUNT + x) * 2 + core


def fan_out(value, axis, pair_sets):
    total = None
    for pairs in pair_sets:
        moved = lax.ppermute(value, axis, pairs)
        total = moved if total is None else total + moved
    return total


def share_planes(mine, row):
    core = row % 2
    x = (row // 2) % X_COUNT
    z = row // (2 * X_COUNT)
    first = fan_out(
        mine,
        "row",
        [[(row_of(0, 0, 0), row_of(k, 0, 0)), (row_of(0, 0, 1), row_of(0, k, 1))] for k in (1, 3, 2)],
    )
    held = jnp.where(row < 2, mine, first)
    second = fan_out(
        held,
        "row",
        [
            [(row_of(z, 0, 0), row_of(z, k, 0)) for z in range(Z_COUNT)]
            + [(row_of(0, x, 1), row_of(k, x, 1)) for x in range(X_COUNT)]
            for k in (1, 3, 2)
        ],
    )
    holder = jnp.where(core == 0, x, z) == 0
    final = jnp.where(holder, held, second)
    other = lax.ppermute(final, "row", [(r, r ^ 1) for r in range(2 * X_COUNT * Z_COUNT)])
    return final, other


def share_row(value, root, col):
    right, left, far = (root + 1) % COLS, (root + 3) % COLS, (root + 2) % COLS
    one = lax.ppermute(value, "col", [(root, right)])
    held = jnp.where(col == root, value, one)
    two = lax.ppermute(held, "col", [(root, left), (right, far)])
    return jnp.where((col == root) | (col == right), held, two)


def share_pivots(value, roots):
    return fan_out(
        value,
        ("row", "col"),
        [[(r * COLS + c, r * COLS + (c + k) % COLS) for r, c in roots] for k in (1, 3, 2)],
    )


def body(factor_u, factor_v, near_field, sketch, tile_ranks):
    tile, width = factor_u.shape[4:]
    row = lax.axis_index("row")
    col = lax.axis_index("col")
    core = row % 2
    own_u = factor_u.reshape(2, tile, width)
    own_v = factor_v.reshape(2, tile, width)
    ranks = tile_ranks.reshape(3, -1, 2)
    own_ranks = lax.dynamic_slice_in_dim(ranks, row, 1, 1)[:, 0]
    order = (width - width // 4, width - width // 4 - (width - width // 4) // 4)
    sketch_t = [sketch[k, :, : order[k]].T for k in range(2)]

    def flags_of(panel):
        slots = jnp.arange(2) * 4 + col
        chosen = (row > panel) & (slots > panel)
        if panel == 0:
            chosen = chosen & jnp.logical_not((row == 1) & (slots == 1))
        lower = (row > col) & (col < 2)
        pivot = (row == col) & (col < 2)
        parts = [own_ranks[panel + 1], own_ranks[0], ranks[0, 0], chosen]
        parts += [lower[None], pivot[None], col[None], core[None]]
        return jnp.concatenate([part.astype(jnp.int32) for part in parts])

    flags = [flags_of(panel) for panel in range(2)]
    one, pair = (tile, width), (2, tile, width)

    with jax.named_scope("first_share"):
        keep = jnp.arange(width, dtype=jnp.int32) < own_ranks[0, 0]
        pack = jnp.where(keep, jnp.stack([own_u[0], own_v[0]]), 0.0)
        got = share_pivots(pack, [(0, 0), (1, 1)])
        corner = jnp.where(col == row, pack, got)
        ours_v, theirs_v = share_planes(jnp.where(core == 0, own_v, pack), row)
    with jax.named_scope("first_upper"):
        up_a, up_b = call(functools.partial(upper_kernel, 0), (one, one), flags[0], near_field, corner, own_u)
    with jax.named_scope("first_lead"):
        held, _ = lax.optimization_barrier((pack, got))
        lead = share_row(held, 0, col)
    with jax.named_scope("upper_share"):
        crossed = lax.ppermute(up_b, "row", [(0, 1)])
        up_a, up_b = share_planes(jnp.where(core == 0, up_a, crossed), row)
    with jax.named_scope("first_wide"):
        wide, extra = call(wide_kernel, (pair, pair), flags[0], lead, up_a, up_b, ours_v, theirs_v)
        got = share_pivots(extra, [(1, 1)])
        extra = jnp.where(col == row, extra, got)
    with jax.named_scope("first_update"):
        scratch = [[pltpu.VMEM((2, width, tile), F32), pltpu.VMEM((2, order[k], width), F32)] for k in range(2)]
        cur_u, cur_v, pack = call(
            functools.partial(panel_kernel, order[0], True),
            (pair, pair, pair),
            flags[0], own_u, own_v, wide, ours_v, theirs_v, sketch_t[0],
            scratch=scratch[0],
        )
    with jax.named_scope("second_upper"):
        fresh = call(functools.partial(upper_kernel, 1), (pair,), flags[1], near_field, corner, extra, cur_u)
    with jax.named_scope("second_share"):
        crossed = lax.ppermute(fresh, "row", [(1, 0)])
        fresh_a, fresh_b = share_planes(jnp.where(core == 1, cur_v, crossed), row)
        lead = share_row(pack, 1, col)
    with jax.named_scope("lower"):
        low = call(
            lower_kernel, ((width, tile),),
            flags[1], near_field, up_a, up_b, ours_v, theirs_v, fresh_a, fresh_b, cur_v,
        )
    with jax.named_scope("second_update"):
        cur_u, cur_v = call(
            functools.partial(panel_kernel, order[1], False),
            (pair, pair),
            flags[1], cur_u, cur_v, lead, fresh_a, fresh_b, low, sketch_t[1],
            scratch=scratch[1],
        )
    shape_out = factor_u.shape
    return cur_u.reshape(shape_out), cur_v.reshape(shape_out)


def solution(mesh):
    tiles = P(None, "row", None, "col", None, None)
    return jax.shard_map(
        body,
        mesh=mesh,
        in_specs=(tiles, tiles, P(), P(), P(None, None, None, None, "col")),
        out_specs=(tiles, tiles),
        check_vma=False,
    )
```

```python
import functools
import math
import jax
import jax.numpy as jnp
from jax import lax
from jax.experimental import pallas as pl
from jax.experimental.pallas import tpu as pltpu
from jax.sharding import PartitionSpec as P

F32 = jnp.float32
BF16 = jnp.bfloat16
NN = (((1,), (0,)), ((), ()))
NT = (((1,), (1,)), ((), ()))
TN = (((0,), (0,)), ((), ()))


def dot6(a, b, dims=NN):
    return lax.dot_general(a, b, dims, precision=lax.Precision.HIGHEST, preferred_element_type=F32)


def split(a):
    high = a.astype(BF16)
    return high, (a - high.astype(F32)).astype(BF16)


def dot1(a, b, dims=NN):
    return lax.dot_general(a, b, dims, preferred_element_type=F32)


def dot3(a, b, dims=NN):
    ah, al = a if isinstance(a, tuple) else split(a)
    bh, bl = b if isinstance(b, tuple) else split(b)
    return dot1(ah, bh, dims) + (dot1(ah, bl, dims) + dot1(al, bh, dims))


def iota(shape, axis):
    return lax.broadcasted_iota(jnp.int32, shape, axis)


def eliminate(grams, order):
    count = len(grams)
    lane8 = iota((8, 128), 1)
    row8 = iota((8, 128), 0)
    blocks = [[g[8 * b:8 * b + 8, :] for b in range(order // 8)] for g in grams]
    done = [[] for _ in grams]
    for step in range(order // 8):
        base = 8 * step
        panels, pivots_all = [], []
        for g in range(count):
            panel = blocks[g][step]
            cols = [jnp.broadcast_to(panel[:, base + c:base + c + 1], (8, 128)) for c in range(8)]
            inside = (lane8 >= base) & (lane8 < base + 8)
            work = jnp.where(inside, (lane8 - base == row8).astype(F32), panel)
            scale = jnp.zeros((8, 128), F32)
            for c in range(8):
                pivot = jnp.broadcast_to(cols[c][c:c + 1, :], (8, 128))
                inverse = 1.0 / pivot
                scale = jnp.where(row8 == c, inverse, scale)
                if c < 7:
                    factor = jnp.where(row8 > c, cols[c] * inverse, 0.0)
                    for d in range(c + 1, 8):
                        cols[d] = cols[d] - factor * jnp.broadcast_to(cols[d][c:c + 1, :], (8, 128))
                    work = work - factor * jnp.broadcast_to(work[c:c + 1, :], (8, 128))
            panels.append(work)
            pivots_all.append(scale)
        for g in range(count):
            work, scale = panels[g], pivots_all[g]
            done[g].append(work * jnp.sqrt(scale))
            if step + 1 < order // 8:
                update = dot6(work, work * scale, TN)
                inside = (lane8 >= base) & (lane8 < base + 8)
                for b in range(step + 1, order // 8):
                    blocks[g][b] = jnp.where(inside, 0.0, blocks[g][b]) - update[8 * b:8 * b + 8, :]
    outs = []
    for g in range(count):
        full = jnp.concatenate(done[g], axis=0)
        keep = iota((order, 128), 1) <= iota((order, 128), 0)
        outs.append(jnp.where(keep, full, 0.0))
    return outs


def wide_t(lead, z_t):
    weight = 1.0 / (8.0 * lead.shape[1])
    core_t = weight * dot3(z_t, lead[1])
    return core_t


def diagonal_inverse(far):
    eye = iota(far.shape, 0) == iota(far.shape, 1)
    return 1.0 / jnp.sum(jnp.where(eye, far, 0.0), axis=0, keepdims=True)


def series(pivot, start):
    eye = iota(pivot.shape, 0) == iota(pivot.shape, 1)
    rest = split(jnp.where(eye, 1.0, 0.0) - pivot * start)
    square = split(dot3(rest, rest))
    return rest, square, split(dot3(square, square))


def upper_kernel(flags, near, corner, own_u, own_v, out_a, out_b):
    tile, width = own_u.shape[1:]
    weight = 1.0 / (8.0 * tile)
    far = near[0]
    start = diagonal_inverse(far)
    parts = series(far + weight * dot3(corner[0], corner[1], NT), start)
    lanes = iota((tile, width), 1)
    values = jnp.concatenate([jnp.where(lanes < flags[2 + s], own_u[s], 0.0).T for s in range(2)], axis=0)
    for part in parts[::-1]:
        values = values + dot3(values, part, NT)
    values = values * start
    out_a[:width] = jnp.where(flags[10] == 0, corner[0].T, values[:width])
    out_a[width:] = own_v[0].T
    out_b[:width] = values[width:]
    out_b[width:] = own_v[1].T


def wide_kernel(flags, lead, crossed, out):
    width = lead.shape[2]
    out[:width] = dot3(wide_t(lead, crossed[:width]), lead[0], NT)
    out[width:] = crossed[width:]


def panel_kernel(order, panel, flags, near, cu, cv, lead, ours, theirs, *refs):
    if panel == 0:
        corner, extra, sketch, nu, nv, pack, out_z, out_v, ortho, factor, moved = refs
    else:
        ours_0, theirs_0, sketch, nu, nv, ortho, factor, moved = refs
    tile, width = cu.shape[1:]
    weight = 1.0 / (8.0 * tile)
    root = math.sqrt(tile)
    lanes = iota((tile, width), 1)
    spare = jnp.zeros((width - order, tile), F32)
    row_g = iota((order, width), 0)
    lane_g = iota((order, width), 1)
    eye = (row_g == lane_g).astype(F32)
    even = flags[11] == 0
    full_us, full_vs, bases, grams, units = [], [], [], [], []
    test_t = sketch[panel].T[:order]
    for s in range(2):
        own_u = cu[s]
        if panel == 0:
            own_u = jnp.where(lanes < flags[2 + s], own_u, 0.0)
            slot = jnp.where(even, theirs[...], ours[...]) if s == 0 else jnp.where(even, ours[...], theirs[...])
            z_t, up_v = slot[:width], slot[width:].T
        else:
            part = ours.shape[1]
            rest = jnp.zeros((width - part, tile), F32)
            z_t = jnp.concatenate([jnp.where(even, ours[s], theirs[s]), rest], axis=0)
            up_v = jnp.concatenate([jnp.where(even, theirs[s], ours[s]), rest], axis=0).T
        side = dot3(lead[0], wide_t(lead, z_t), NT)
        full_u = jnp.concatenate([own_u, -side], axis=1)
        full_v = jnp.concatenate([cv[s], up_v], axis=1)
        projected = dot6(test_t, full_v)
        basis = dot6(projected, full_u, NT)
        basis = jnp.where(iota((order, tile), 0) < flags[s], basis, 0.0)
        basis = jnp.concatenate([basis, spare], axis=0)
        unit = jnp.where((row_g == lane_g) & (row_g >= flags[s]), 1.0, 0.0)
        grams.append(dot6(basis[:order], basis, NT) + unit)
        full_us.append(full_u)
        full_vs.append(full_v)
        bases.append(basis)
        units.append(unit)

    if panel == 0:
        far = near[1]
        start = diagonal_inverse(far)
        low_rank = dot3(corner[0], corner[1], NT) - dot3(extra[:width], extra[width:], TN)
        parts = series(far + weight * low_rank, start)
    else:
        left = flags[10] == 0
        slot = jnp.where(even, theirs_0[...], ours_0[...])
        moved[:part] = jnp.where(even, ours[0], theirs[0])
        moved[part:2 * part] = jnp.where(even, theirs[0], ours[0])
        moved[2 * part:3 * part] = jnp.where(even, ours[2], theirs[2])
        moved[3 * part:] = jnp.where(even, theirs[2], ours[2])
        far = jnp.where(left, near[0], near[1])
        start = diagonal_inverse(far)
        one_u = jnp.where(left, slot[:width], moved[width:2 * width])
        one_v = jnp.where(left, slot[width:], moved[2 * width:])
        two_u = jnp.where(left, 0.0, moved[:width])
        low_rank = dot3(one_u, one_v, TN) - dot3(two_u, slot[width:], TN)
        low = cv[0].T * start
        for factors in series(far + weight * low_rank, start):
            low = low + dot3(low, factors)

    inverses = eliminate(grams, order)
    defect = jnp.zeros((), F32)
    for s in range(2):
        once = dot6(inverses[s], bases[s])
        ortho[s, :order] = once
        ortho[s, order:] = spare
        gram = dot6(once, jnp.concatenate([once, spare], axis=0), NT) + units[s]
        factor[s] = gram
        off = gram - eye
        defect = defect + jnp.where(flags[6 + s] == 1, jnp.sum(off * off), 0.0)
    near_unit = defect < 1e-6

    @pl.when(near_unit)
    def _():
        for s in range(2):
            off = factor[s] - eye
            half = jnp.where(lane_g < row_g, off, jnp.where(lane_g == row_g, 0.5 * off, 0.0))
            once = ortho[s]
            ortho[s, :order] = once[:order] - dot1(half.astype(BF16), once.astype(BF16))

    @pl.when(jnp.logical_not(near_unit))
    def _():
        again = eliminate([factor[0], factor[1]], order)
        for s in range(2):
            ortho[s, :order] = dot6(again[s], ortho[s])

    fresh_vs = []
    for s in range(2):
        basis = ortho[s]
        back = dot3(basis, full_us[s])
        fresh_v = dot3(full_vs[s], back, NT) * (1.0 / root)
        fresh_u = basis.T * root
        fresh_vs.append(fresh_v)
        keep_u = cu[s]
        keep_v = cv[s]
        if panel == 0:
            keep_u = jnp.where(lanes < flags[2 + s], keep_u, 0.0)
            keep_v = jnp.where(lanes < flags[2 + s], keep_v, 0.0)
        elif s == 0:
            keep_v = jnp.where(flags[8] == 1, low.T, keep_v)
            keep_u = jnp.where(flags[9] == 1, 0.0, keep_u)
            keep_v = jnp.where(flags[9] == 1, 0.0, keep_v)
        chosen = flags[6 + s] == 1
        new_u = jnp.where(chosen, fresh_u, keep_u)
        new_v = jnp.where(chosen, fresh_v, keep_v)
        nu[s] = new_u
        nv[s] = new_v
        if panel == 0 and s == 0:
            pack[0] = new_u
            pack[1] = new_v
    if panel == 0:
        values = jnp.concatenate([ortho[0, :order], ortho[1, :order]], axis=0) * root
        for factors in parts[::-1]:
            values = values + dot3(values, factors, NT)
        values = values * start
        moved[:width] = extra[:width]
        moved[width:2 * width] = corner[0].T
        moved[2 * width:] = corner[1].T
        middle = flags[10] == 1
        out_z[0] = jnp.where(middle, moved[:order], values[:order])
        out_z[1] = values[order:]
        out_z[2] = moved[2 * order:3 * order]
        out_v[0] = jnp.where(middle, moved[order:2 * order], fresh_vs[0].T[:order])
        out_v[1] = fresh_vs[1].T[:order]
        out_v[2] = moved[3 * order:]


def call(kernel, shapes, flags, *values, scratch=()):
    vmem = pl.BlockSpec(memory_space=pltpu.VMEM)
    shapes = tuple(jax.ShapeDtypeStruct(shape, F32) for shape in shapes)
    out = pl.pallas_call(
        kernel,
        out_shape=shapes,
        in_specs=[pl.BlockSpec(memory_space=pltpu.SMEM)] + [vmem] * len(values),
        out_specs=(vmem,) * len(shapes),
        scratch_shapes=list(scratch),
        compiler_params=pltpu.CompilerParams(vmem_limit_bytes=32 * 1024 * 1024),
    )(flags, *values)
    return out if len(out) > 1 else out[0]


Z_COUNT = 4
X_COUNT = 4
COLS = 4


def row_of(z, x, core):
    return (z * X_COUNT + x) * 2 + core


def fan_out(value, axis, pair_sets):
    total = None
    for pairs in pair_sets:
        moved = lax.ppermute(value, axis, pairs)
        total = moved if total is None else total + moved
    return total


def share_planes(mine, row):
    core = row % 2
    x = (row // 2) % X_COUNT
    z = row // (2 * X_COUNT)
    first = fan_out(
        mine,
        "row",
        [[(row_of(0, 0, 0), row_of(k, 0, 0)), (row_of(0, 0, 1), row_of(0, k, 1))] for k in (1, 3, 2)],
    )
    held = jnp.where(row < 2, mine, first)
    second = fan_out(
        held,
        "row",
        [
            [(row_of(z, 0, 0), row_of(z, k, 0)) for z in range(Z_COUNT)]
            + [(row_of(0, x, 1), row_of(k, x, 1)) for x in range(X_COUNT)]
            for k in (1, 3, 2)
        ],
    )
    holder = jnp.where(core == 0, x, z) == 0
    final = jnp.where(holder, held, second)
    other = lax.ppermute(final, "row", [(r, r ^ 1) for r in range(2 * X_COUNT * Z_COUNT)])
    return final, other


def share_row(value, root, col):
    right, left, far = (root + 1) % COLS, (root + 3) % COLS, (root + 2) % COLS
    one = lax.ppermute(value, "col", [(root, right)])
    held = jnp.where(col == root, value, one)
    two = lax.ppermute(held, "col", [(root, left), (right, far)])
    return held, jnp.where((col == root) | (col == right), held, two)


def share_pivots(value, roots):
    return fan_out(
        value,
        ("row", "col"),
        [[(r * COLS + c, r * COLS + (c + k) % COLS) for r, c in roots] for k in (1, 3, 2)],
    )


def body(factor_u, factor_v, near_field, sketch, tile_ranks):
    tile, width = factor_u.shape[4:]
    row = lax.axis_index("row")
    col = lax.axis_index("col")
    core = row % 2
    own_u = factor_u.reshape(2, tile, width)
    own_v = factor_v.reshape(2, tile, width)
    ranks = tile_ranks.reshape(3, -1, 2)
    own_ranks = lax.dynamic_slice_in_dim(ranks, row, 1, 1)[:, 0]
    order = (width - width // 4, width - width // 4 - (width - width // 4) // 4)

    def flags_of(panel):
        slots = jnp.arange(2) * 4 + col
        chosen = (row > panel) & (slots > panel)
        if panel == 0:
            chosen = chosen & jnp.logical_not((row == 1) & (slots == 1))
        lower = (row > col) & (col < 2)
        pivot = (row == col) & (col < 2)
        parts = [own_ranks[panel + 1], own_ranks[0], ranks[0, 0], chosen]
        parts += [lower[None], pivot[None], col[None], core[None]]
        return jnp.concatenate([part.astype(jnp.int32) for part in parts])

    flags = [flags_of(panel) for panel in range(2)]
    pair, payload = (2, tile, width), (2 * width, tile)
    packed = (3, order[0], tile)
    scratch = [
        [pltpu.VMEM(pair[:1] + (width, tile), F32), pltpu.VMEM((2, order[k], width), F32), pltpu.VMEM((4 * order[0], tile), F32)]
        for k in range(2)
    ]

    with jax.named_scope("corner_share"):
        pack = jnp.stack([own_u[0], own_v[0]])
        got = share_pivots(pack, [(0, 0), (1, 1)])
        corner = jnp.where(col == row, pack, got)
    with jax.named_scope("first_lead"):
        keep = jnp.arange(width, dtype=jnp.int32) < own_ranks[0, 0]
        near_lead, lead = share_row(jnp.where(keep, pack, 0.0), 0, col)
    with jax.named_scope("first_upper"):
        up_a, up_b = call(upper_kernel, (payload, payload), flags[0], near_field, corner, own_u, own_v)
    with jax.named_scope("upper_share"):
        crossed = lax.ppermute(up_a, "row", [(0, 1)])
        ours_0, theirs_0 = share_planes(jnp.where(core == 0, up_b, crossed), row)
    with jax.named_scope("wide_share"):
        extra = call(wide_kernel, (payload,), flags[0], near_lead, crossed)
        got = share_pivots(extra, [(1, 1)])
        extra = jnp.where(col == row, extra, got)
    with jax.named_scope("first_update"):
        cur_u, cur_v, pack, out_z, out_v = call(
            functools.partial(panel_kernel, order[0], 0),
            (pair, pair, pair, packed, packed),
            flags[0], near_field, own_u, own_v, lead, ours_0, theirs_0, corner, extra, sketch,
            scratch=scratch[0],
        )
    with jax.named_scope("second_share"):
        _, lead = share_row(pack, 1, col)
        crossed = lax.ppermute(out_z, "row", [(1, 0)])
        ours, theirs = share_planes(jnp.where(core == 1, out_v, crossed), row)
    with jax.named_scope("second_update"):
        cur_u, cur_v = call(
            functools.partial(panel_kernel, order[1], 1),
            (pair, pair),
            flags[1], near_field, cur_u, cur_v, lead, ours, theirs, ours_0, theirs_0, sketch,
            scratch=scratch[1],
        )
    shape_out = factor_u.shape
    return cur_u.reshape(shape_out), cur_v.reshape(shape_out)


def solution(mesh):
    tiles = P(None, "row", None, "col", None, None)
    return jax.shard_map(
        body,
        mesh=mesh,
        in_specs=(tiles, tiles, P(), P(), P(None, None, None, None, "col")),
        out_specs=(tiles, tiles),
        check_vma=False,
    )
```

```python
import functools
import math
import jax
import jax.numpy as jnp
from jax import lax
from jax.experimental import pallas as pl
from jax.experimental.pallas import tpu as pltpu
from jax.sharding import PartitionSpec as P

F32 = jnp.float32
BF16 = jnp.bfloat16
NN = (((1,), (0,)), ((), ()))
NT = (((1,), (1,)), ((), ()))
TN = (((0,), (0,)), ((), ()))


def dot6(a, b, dims=NN):
    return lax.dot_general(a, b, dims, precision=lax.Precision.HIGHEST, preferred_element_type=F32)


def split(a):
    high = a.astype(BF16)
    return high, (a - high.astype(F32)).astype(BF16)


def dot1(a, b, dims=NN):
    return lax.dot_general(a, b, dims, preferred_element_type=F32)


def dot3(a, b, dims=NN):
    ah, al = a if isinstance(a, tuple) else split(a)
    bh, bl = b if isinstance(b, tuple) else split(b)
    return dot1(ah, bh, dims) + (dot1(ah, bl, dims) + dot1(al, bh, dims))


def iota(shape, axis):
    return lax.broadcasted_iota(jnp.int32, shape, axis)


def eliminate(grams, order):
    count = len(grams)
    lane8 = iota((8, 128), 1)
    row8 = iota((8, 128), 0)
    blocks = [[g[8 * b:8 * b + 8, :] for b in range(order // 8)] for g in grams]
    done = [[] for _ in grams]
    for step in range(order // 8):
        base = 8 * step
        panels, pivots_all = [], []
        for g in range(count):
            panel = blocks[g][step]
            cols = [jnp.broadcast_to(panel[:, base + c:base + c + 1], (8, 128)) for c in range(8)]
            inside = (lane8 >= base) & (lane8 < base + 8)
            work = jnp.where(inside, (lane8 - base == row8).astype(F32), panel)
            scale = jnp.zeros((8, 128), F32)
            for c in range(8):
                pivot = jnp.broadcast_to(cols[c][c:c + 1, :], (8, 128))
                inverse = 1.0 / pivot
                scale = jnp.where(row8 == c, inverse, scale)
                if c < 7:
                    factor = jnp.where(row8 > c, cols[c] * inverse, 0.0)
                    for d in range(c + 1, 8):
                        cols[d] = cols[d] - factor * jnp.broadcast_to(cols[d][c:c + 1, :], (8, 128))
                    work = work - factor * jnp.broadcast_to(work[c:c + 1, :], (8, 128))
            panels.append(work)
            pivots_all.append(scale)
        for g in range(count):
            work, scale = panels[g], pivots_all[g]
            done[g].append(work * jnp.sqrt(scale))
            if step + 1 < order // 8:
                update = dot6(work, work * scale, TN)
                inside = (lane8 >= base) & (lane8 < base + 8)
                for b in range(step + 1, order // 8):
                    blocks[g][b] = jnp.where(inside, 0.0, blocks[g][b]) - update[8 * b:8 * b + 8, :]
    outs = []
    for g in range(count):
        full = jnp.concatenate(done[g], axis=0)
        keep = iota((order, 128), 1) <= iota((order, 128), 0)
        outs.append(jnp.where(keep, full, 0.0))
    return outs


def diagonal_inverse(far):
    eye = iota(far.shape, 0) == iota(far.shape, 1)
    return 1.0 / jnp.sum(jnp.where(eye, far, 0.0), axis=0, keepdims=True)


def series(pivot, start):
    eye = iota(pivot.shape, 0) == iota(pivot.shape, 1)
    rest = split(jnp.where(eye, 1.0, 0.0) - pivot * start)
    square = split(dot3(rest, rest))
    return rest, square, split(dot3(square, square))


def lower_kernel(flags, near, ours, theirs, own_v, out, up):
    tile, width = ours.shape
    weight = 1.0 / (8.0 * tile)
    even = flags[11] == 0
    lanes = iota((tile, width), 1)
    up_u = jnp.where(even, ours[...], theirs[...])
    up_v = jnp.where(even, theirs[...], ours[...])
    up[0] = jnp.where(lanes < flags[4], up_u, 0.0)
    up[1] = up_v
    far = near[0]
    start = diagonal_inverse(far)
    low = jnp.where(lanes < flags[2], own_v[0], 0.0).T * start
    for part in series(far + weight * dot3(up_u, up_v, NT), start):
        low = low + dot3(low, part)
    out[...] = low


def panel_kernel(order, panel, flags, near, cu, cv, lead, ours, theirs, *refs):
    if panel == 0:
        ours_1, theirs_1, low_t, corner, cross, sketch, nu, nv, pack, out_z, out_v, ortho, factor, moved = refs
    else:
        ours_0, theirs_0, sketch, nu, nv, ortho, factor, moved = refs
    tile, width = cu.shape[1:]
    weight = 1.0 / (8.0 * tile)
    root = math.sqrt(tile)
    lanes = iota((tile, width), 1)
    spare = jnp.zeros((width - order, tile), F32)
    row_g = iota((order, width), 0)
    lane_g = iota((order, width), 1)
    eye = (row_g == lane_g).astype(F32)
    even = flags[11] == 0
    full_us, full_vs, bases, grams, units = [], [], [], [], []
    test_t = sketch[panel].T[:order]
    if panel == 1:
        part = ours.shape[1]
        rest = jnp.zeros((width - part, tile), F32)
        lead_u = jnp.concatenate([lead[0], rest], axis=0)
        lead_v = jnp.concatenate([lead[1], rest], axis=0)
    for s in range(2):
        own_u = cu[s]
        if panel == 0:
            own_u = jnp.where(lanes < flags[2 + s], own_u, 0.0)
            mine, other = ((ours, theirs), (ours_1, theirs_1))[s]
            up_u = jnp.where(even, mine[...], other[...])
            up_u = jnp.where(lanes < flags[4 + s], up_u, 0.0)
            up_v = jnp.where(even, other[...], mine[...])
            side = dot3(lead[...], weight * dot3(low_t[...], up_u))
        else:
            z_t = jnp.concatenate([jnp.where(even, ours[s], theirs[s]), rest], axis=0)
            up_v = jnp.concatenate([jnp.where(even, theirs[s], ours[s]), rest], axis=0).T
            side = dot3(weight * dot3(z_t, lead_v, NT), lead_u).T
        full_u = jnp.concatenate([own_u, -side], axis=1)
        full_v = jnp.concatenate([cv[s], up_v], axis=1)
        projected = dot6(test_t, full_v)
        basis = dot6(projected, full_u, NT)
        basis = jnp.where(iota((order, tile), 0) < flags[s], basis, 0.0)
        basis = jnp.concatenate([basis, spare], axis=0)
        unit = jnp.where((row_g == lane_g) & (row_g >= flags[s]), 1.0, 0.0)
        grams.append(dot6(basis[:order], basis, NT) + unit)
        full_us.append(full_u)
        full_vs.append(full_v)
        bases.append(basis)
        units.append(unit)

    far = near[1]
    start = diagonal_inverse(far)
    if panel == 0:
        wide = dot3(lead[...], weight * dot3(low_t[...], cross[0]))
        low_rank = dot3(corner[0], corner[1], NT) - dot3(wide, cross[1], NT)
        parts = series(far + weight * low_rank, start)
    else:
        moved[:part] = jnp.where(even, ours[0], theirs[0])
        moved[part:2 * part] = jnp.where(even, theirs[0], ours[0])
        moved[2 * part:3 * part] = jnp.where(even, ours[2], theirs[2])
        moved[3 * part:] = jnp.where(even, theirs[2], ours[2])
        first_v = jnp.where(even, theirs_0[...], ours_0[...]).T
        low_rank = dot3(moved[width:2 * width], moved[2 * width:], TN) - dot3(moved[:width], first_v, TN)
        low = cv[0].T * start
        for factors in series(far + weight * low_rank, start):
            low = low + dot3(low, factors)

    inverses = eliminate(grams, order)
    defect = jnp.zeros((), F32)
    for s in range(2):
        once = dot6(inverses[s], bases[s])
        ortho[s, :order] = once
        ortho[s, order:] = spare
        gram = dot3(once, jnp.concatenate([once, spare], axis=0), NT) + units[s]
        factor[s] = gram
        off = gram - eye
        defect = defect + jnp.where(flags[6 + s] == 1, jnp.sum(off * off), 0.0)
    near_unit = defect < 1e-6

    @pl.when(near_unit)
    def _():
        for s in range(2):
            off = factor[s] - eye
            half = jnp.where(lane_g < row_g, off, jnp.where(lane_g == row_g, 0.5 * off, 0.0))
            once = ortho[s]
            ortho[s, :order] = once[:order] - dot1(half.astype(BF16), once.astype(BF16))

    @pl.when(jnp.logical_not(near_unit))
    def _():
        again = eliminate([factor[0], factor[1]], order)
        for s in range(2):
            ortho[s, :order] = dot6(again[s], ortho[s])

    fresh_vs = []
    for s in range(2):
        basis = ortho[s]
        back = dot3(basis, full_us[s])
        fresh_v = dot3(full_vs[s], back, NT) * (1.0 / root)
        fresh_u = basis.T * root
        fresh_vs.append(fresh_v)
        keep_u = cu[s]
        keep_v = cv[s]
        if panel == 0:
            keep_u = jnp.where(lanes < flags[2 + s], keep_u, 0.0)
            keep_v = jnp.where(lanes < flags[2 + s], keep_v, 0.0)
        if s == 0:
            keep_v = jnp.where(flags[8] == 1, (low_t[...] if panel == 0 else low).T, keep_v)
            keep_u = jnp.where(flags[9] == 1, 0.0, keep_u)
            keep_v = jnp.where(flags[9] == 1, 0.0, keep_v)
        chosen = flags[6 + s] == 1
        new_u = jnp.where(chosen, fresh_u, keep_u)
        new_v = jnp.where(chosen, fresh_v, keep_v)
        nu[s] = new_u
        nv[s] = new_v
    if panel == 0:
        values = jnp.concatenate([ortho[0, :order], ortho[1, :order]], axis=0) * root
        for factors in parts[::-1]:
            values = values + dot3(values, factors, NT)
        values = values * start
        moved[:width] = wide.T
        moved[width:2 * width] = corner[0].T
        moved[2 * width:] = corner[1].T
        middle = flags[10] == 1
        fresh_t = fresh_vs[0].T[:order]
        pack[0] = ortho[0, :order] * root
        pack[1] = fresh_t
        out_z[0] = jnp.where(middle, moved[:order], values[:order])
        out_z[1] = values[order:]
        out_z[2] = moved[2 * order:3 * order]
        out_v[0] = jnp.where(middle, moved[order:2 * order], fresh_t)
        out_v[1] = fresh_vs[1].T[:order]
        out_v[2] = moved[3 * order:]


def call(kernel, shapes, flags, *values, scratch=()):
    vmem = pl.BlockSpec(memory_space=pltpu.VMEM)
    shapes = tuple(jax.ShapeDtypeStruct(shape, F32) for shape in shapes)
    out = pl.pallas_call(
        kernel,
        out_shape=shapes,
        in_specs=[pl.BlockSpec(memory_space=pltpu.SMEM)] + [vmem] * len(values),
        out_specs=(vmem,) * len(shapes),
        scratch_shapes=list(scratch),
        compiler_params=pltpu.CompilerParams(vmem_limit_bytes=24 * 1024 * 1024),
    )(flags, *values)
    return out if len(out) > 1 else out[0]


Z_COUNT = 4
X_COUNT = 4
COLS = 4


def row_of(z, x, core):
    return (z * X_COUNT + x) * 2 + core


def fan_out(value, axis, pair_sets):
    total = None
    for pairs in pair_sets:
        moved = lax.ppermute(value, axis, pairs)
        total = moved if total is None else total + moved
    return total


def share_planes(mine, row):
    core = row % 2
    x = (row // 2) % X_COUNT
    z = row // (2 * X_COUNT)
    first = fan_out(
        mine,
        "row",
        [[(row_of(0, 0, 0), row_of(k, 0, 0)), (row_of(0, 0, 1), row_of(0, k, 1))] for k in (1, 3, 2)],
    )
    held = jnp.where(row < 2, mine, first)
    second = fan_out(
        held,
        "row",
        [
            [(row_of(z, 0, 0), row_of(z, k, 0)) for z in range(Z_COUNT)]
            + [(row_of(0, x, 1), row_of(k, x, 1)) for x in range(X_COUNT)]
            for k in (1, 3, 2)
        ],
    )
    holder = jnp.where(core == 0, x, z) == 0
    final = jnp.where(holder, held, second)
    other = lax.ppermute(final, "row", [(r, r ^ 1) for r in range(2 * X_COUNT * Z_COUNT)])
    return final, other, second


def share_row(value, root, col):
    right, left, far = (root + 1) % COLS, (root + 3) % COLS, (root + 2) % COLS
    one = lax.ppermute(value, "col", [(root, right)])
    held = jnp.where(col == root, value, one)
    two = lax.ppermute(held, "col", [(root, left), (right, far)])
    return jnp.where((col == root) | (col == right), held, two)


def fan_row(value, root, col):
    got = fan_out(value, "col", [[(root, (root + k) % COLS)] for k in (1, 3, 2)])
    return jnp.where(col == root, value, got)


def share_pivot(value, col):
    got = fan_out(value, ("row", "col"), [[(COLS + 1, COLS + (1 + k) % COLS)] for k in (1, 3, 2)])
    return jnp.where(col == 1, value, got)


def body(factor_u, factor_v, near_field, sketch, tile_ranks):
    tile, width = factor_u.shape[4:]
    row = lax.axis_index("row")
    col = lax.axis_index("col")
    core = row % 2
    own_u = factor_u.reshape(2, tile, width)
    own_v = factor_v.reshape(2, tile, width)
    ranks = tile_ranks.reshape(3, -1, 2)
    own_ranks = lax.dynamic_slice_in_dim(ranks, row, 1, 1)[:, 0]
    order = (width - width // 4, width - width // 4 - (width - width // 4) // 4)

    def flags_of(panel):
        slots = jnp.arange(2) * 4 + col
        chosen = (row > panel) & (slots > panel)
        if panel == 0:
            chosen = chosen & jnp.logical_not((row == 1) & (slots == 1))
        lower = (row > panel) & (col == panel)
        pivot = (row == panel) & (col == panel)
        parts = [own_ranks[panel + 1], own_ranks[0], ranks[0, 0], chosen]
        parts += [lower[None], pivot[None], col[None], core[None]]
        return jnp.concatenate([part.astype(jnp.int32) for part in parts])

    flags = [flags_of(panel) for panel in range(2)]
    one, pair = (tile, width), (2, tile, width)
    packed = (3, order[0], tile)
    scratch = [
        [pltpu.VMEM((2, width, tile), F32), pltpu.VMEM((2, order[k], width), F32), pltpu.VMEM((4 * order[0], tile), F32)]
        for k in range(2)
    ]

    def first_share(slot, after):
        value_u, value_v = own_u[slot], own_v[slot]
        if after is not None:
            value_u, value_v, _ = lax.optimization_barrier((value_u, value_v, after))
        crossed = lax.ppermute(value_v, "row", [(0, 1)])
        return share_planes(jnp.where(core == 0, value_u, crossed), row)

    with jax.named_scope("first_share"):
        ours_0, theirs_0, middle = first_share(0, None)
        lead = share_row(own_u[0], 0, col)
        corner = share_pivot(jnp.stack([own_u[0], own_v[0]]), col)
    with jax.named_scope("first_lower"):
        low_t, cross = call(lower_kernel, ((width, tile), pair), flags[0], near_field, ours_0, theirs_0, own_v)
        low_t = fan_row(low_t, 0, col)
        cross = share_pivot(cross, col)
        ours_1, theirs_1, _ = first_share(1, middle)
    with jax.named_scope("first_update"):
        cur_u, cur_v, pack, out_z, out_v = call(
            functools.partial(panel_kernel, order[0], 0),
            (pair, pair, (2, order[0], tile), packed, packed),
            flags[0], near_field, own_u, own_v, lead, ours_0, theirs_0, ours_1, theirs_1, low_t, corner, cross, sketch,
            scratch=scratch[0],
        )
    with jax.named_scope("second_share"):
        lead = share_row(pack, 1, col)
        crossed = lax.ppermute(out_z, "row", [(1, 0)])
        ours, theirs, _ = share_planes(jnp.where(core == 1, out_v, crossed), row)
    with jax.named_scope("second_update"):
        cur_u, cur_v = call(
            functools.partial(panel_kernel, order[1], 1),
            (pair, pair),
            flags[1], near_field, cur_u, cur_v, lead, ours, theirs, ours_0, theirs_0, sketch,
            scratch=scratch[1],
        )
    shape_out = factor_u.shape
    return cur_u.reshape(shape_out), cur_v.reshape(shape_out)


def solution(mesh):
    tiles = P(None, "row", None, "col", None, None)
    return jax.shard_map(
        body,
        mesh=mesh,
        in_specs=(tiles, tiles, P(), P(), P(None, None, None, None, "col")),
        out_specs=(tiles, tiles),
        check_vma=False,
    )
```

```python
import functools
import math
import jax
import jax.numpy as jnp
from jax import lax
from jax.experimental import pallas as pl
from jax.experimental.pallas import tpu as pltpu
from jax.sharding import PartitionSpec as P

F32 = jnp.float32
BF16 = jnp.bfloat16
NN = (((1,), (0,)), ((), ()))
NT = (((1,), (1,)), ((), ()))
TN = (((0,), (0,)), ((), ()))


def dot6(a, b, dims=NN):
    return lax.dot_general(a, b, dims, precision=lax.Precision.HIGHEST, preferred_element_type=F32)


def split(a):
    high = a.astype(BF16)
    return high, (a - high.astype(F32)).astype(BF16)


def dot1(a, b, dims=NN):
    return lax.dot_general(a, b, dims, preferred_element_type=F32)


def dot3(a, b, dims=NN):
    ah, al = a if isinstance(a, tuple) else split(a)
    bh, bl = b if isinstance(b, tuple) else split(b)
    return dot1(ah, bh, dims) + (dot1(ah, bl, dims) + dot1(al, bh, dims))


def iota(shape, axis):
    return lax.broadcasted_iota(jnp.int32, shape, axis)


def eliminate(grams, order):
    count = len(grams)
    lane8 = iota((8, 128), 1)
    row8 = iota((8, 128), 0)
    blocks = [[g[8 * b:8 * b + 8, :] for b in range(order // 8)] for g in grams]
    done = [[] for _ in grams]
    for step in range(order // 8):
        base = 8 * step
        panels, pivots_all = [], []
        for g in range(count):
            panel = blocks[g][step]
            cols = [jnp.broadcast_to(panel[:, base + c:base + c + 1], (8, 128)) for c in range(8)]
            inside = (lane8 >= base) & (lane8 < base + 8)
            work = jnp.where(inside, (lane8 - base == row8).astype(F32), panel)
            scale = jnp.zeros((8, 128), F32)
            for c in range(8):
                pivot = jnp.broadcast_to(cols[c][c:c + 1, :], (8, 128))
                inverse = 1.0 / pivot
                scale = jnp.where(row8 == c, inverse, scale)
                if c < 7:
                    factor = jnp.where(row8 > c, cols[c] * inverse, 0.0)
                    for d in range(c + 1, 8):
                        cols[d] = cols[d] - factor * jnp.broadcast_to(cols[d][c:c + 1, :], (8, 128))
                    work = work - factor * jnp.broadcast_to(work[c:c + 1, :], (8, 128))
            panels.append(work)
            pivots_all.append(scale)
        for g in range(count):
            work, scale = panels[g], pivots_all[g]
            done[g].append(work * jnp.sqrt(scale))
            if step + 1 < order // 8:
                update = dot6(work, work * scale, TN)
                inside = (lane8 >= base) & (lane8 < base + 8)
                for b in range(step + 1, order // 8):
                    blocks[g][b] = jnp.where(inside, 0.0, blocks[g][b]) - update[8 * b:8 * b + 8, :]
    outs = []
    for g in range(count):
        full = jnp.concatenate(done[g], axis=0)
        keep = iota((order, 128), 1) <= iota((order, 128), 0)
        outs.append(jnp.where(keep, full, 0.0))
    return outs


def wide_t(lead, z_t):
    weight = 1.0 / (8.0 * lead.shape[1])
    core_t = weight * dot3(z_t, lead[1])
    return core_t


def diagonal_inverse(far):
    eye = iota(far.shape, 0) == iota(far.shape, 1)
    return 1.0 / jnp.sum(jnp.where(eye, far, 0.0), axis=0, keepdims=True)


def series(pivot, start):
    eye = iota(pivot.shape, 0) == iota(pivot.shape, 1)
    rest = split(jnp.where(eye, 1.0, 0.0) - pivot * start)
    square = split(dot3(rest, rest))
    return rest, square, split(dot3(square, square))


def upper_kernel(flags, near, corner, own_u, own_v, out_a, out_b):
    tile, width = own_u.shape[1:]
    weight = 1.0 / (8.0 * tile)
    far = near[0]
    start = diagonal_inverse(far)
    parts = series(far + weight * dot3(corner[0], corner[1], NT), start)
    lanes = iota((tile, width), 1)
    values = jnp.concatenate([jnp.where(lanes < flags[2 + s], own_u[s], 0.0).T for s in range(2)], axis=0)
    for part in parts[::-1]:
        values = values + dot3(values, part, NT)
    values = values * start
    out_a[:width] = jnp.where(flags[10] == 0, corner[0].T, values[:width])
    out_a[width:] = own_v[0].T
    out_b[:width] = values[width:]
    out_b[width:] = own_v[1].T


def wide_kernel(flags, lead, crossed, out):
    width = lead.shape[2]
    out[:width] = dot3(wide_t(lead, crossed[:width]), lead[0], NT)
    out[width:] = crossed[width:]


def panel_kernel(order, panel, flags, far_u, far_v, far_near, far_sketch, lead, ours, theirs, *refs):
    if panel == 0:
        corner, extra, to_u, to_v, pack, out_z, out_v = refs[:7]
    else:
        ours_0, theirs_0, to_u, to_v = refs[:4]
    ortho, factor, moved, cu, cv, near, sketch, nu, nv, sems = refs[-10:]
    near_from = far_near.at[1] if panel == 0 else far_near
    loads = [
        pltpu.make_async_copy(far_v, cv, sems.at[0]),
        pltpu.make_async_copy(far_sketch.at[panel], sketch, sems.at[1]),
        pltpu.make_async_copy(far_u, cu, sems.at[2]),
        pltpu.make_async_copy(near_from, near, sems.at[3]),
    ]
    for load in loads:
        load.start()
    tile, width = cu.shape[1:]
    weight = 1.0 / (8.0 * tile)
    root = math.sqrt(tile)
    lanes = iota((tile, width), 1)
    spare = jnp.zeros((width - order, tile), F32)
    row_g = iota((order, width), 0)
    lane_g = iota((order, width), 1)
    eye = (row_g == lane_g).astype(F32)
    even = flags[11] == 0
    full_us, full_vs, bases, grams, units = [], [], [], [], []
    if panel == 1:
        part = ours.shape[1]
        rest = jnp.zeros((width - part, tile), F32)
        lead_u = jnp.concatenate([lead[0], rest], axis=0)
        lead_v = jnp.concatenate([lead[1], rest], axis=0)
    for load in loads:
        load.wait()
    test_t = sketch[...].T[:order]
    for s in range(2):
        own_u = cu[s]
        if panel == 0:
            own_u = jnp.where(lanes < flags[2 + s], own_u, 0.0)
            slot = jnp.where(even, theirs[...], ours[...]) if s == 0 else jnp.where(even, ours[...], theirs[...])
            up_v = slot[width:].T
            side = dot3(lead[0], wide_t(lead, slot[:width]), NT)
        else:
            z_t = jnp.concatenate([jnp.where(even, ours[s], theirs[s]), rest], axis=0)
            up_v = jnp.concatenate([jnp.where(even, theirs[s], ours[s]), rest], axis=0).T
            side = dot3(weight * dot3(z_t, lead_v, NT), lead_u).T
        full_u = jnp.concatenate([own_u, -side], axis=1)
        full_v = jnp.concatenate([cv[s], up_v], axis=1)
        projected = dot6(test_t, full_v)
        basis = dot6(projected, full_u, NT)
        basis = jnp.where(iota((order, tile), 0) < flags[s], basis, 0.0)
        basis = jnp.concatenate([basis, spare], axis=0)
        unit = jnp.where((row_g == lane_g) & (row_g >= flags[s]), 1.0, 0.0)
        grams.append(dot6(basis[:order], basis, NT) + unit)
        full_us.append(full_u)
        full_vs.append(full_v)
        bases.append(basis)
        units.append(unit)

    if panel == 0:
        far = near[...]
        start = diagonal_inverse(far)
        low_rank = dot3(corner[0], corner[1], NT) - dot3(extra[:width], extra[width:], TN)
        parts = series(far + weight * low_rank, start)
    else:
        left = flags[10] == 0
        slot = jnp.where(even, theirs_0[...], ours_0[...])
        moved[:part] = jnp.where(even, ours[0], theirs[0])
        moved[part:2 * part] = jnp.where(even, theirs[0], ours[0])
        moved[2 * part:3 * part] = jnp.where(even, ours[2], theirs[2])
        moved[3 * part:] = jnp.where(even, theirs[2], ours[2])
        far = jnp.where(left, near[0], near[1])
        start = diagonal_inverse(far)
        one_u = jnp.where(left, slot[:width], moved[width:2 * width])
        one_v = jnp.where(left, slot[width:], moved[2 * width:])
        two_u = jnp.where(left, 0.0, moved[:width])
        low_rank = dot3(one_u, one_v, TN) - dot3(two_u, slot[width:], TN)
        low = cv[0].T * start
        for factors in series(far + weight * low_rank, start):
            low = low + dot3(low, factors)

    inverses = eliminate(grams, order)
    defect = jnp.zeros((), F32)
    for s in range(2):
        once = dot6(inverses[s], bases[s])
        ortho[s, :order] = once
        ortho[s, order:] = spare
        gram = dot3(once, jnp.concatenate([once, spare], axis=0), NT) + units[s]
        factor[s] = gram
        off = gram - eye
        defect = defect + jnp.where(flags[6 + s] == 1, jnp.sum(off * off), 0.0)
    near_unit = defect < 1e-6

    @pl.when(near_unit)
    def _():
        for s in range(2):
            off = factor[s] - eye
            half = jnp.where(lane_g < row_g, off, jnp.where(lane_g == row_g, 0.5 * off, 0.0))
            once = ortho[s]
            ortho[s, :order] = once[:order] - dot1(half.astype(BF16), once.astype(BF16))

    @pl.when(jnp.logical_not(near_unit))
    def _():
        again = eliminate([factor[0], factor[1]], order)
        for s in range(2):
            ortho[s, :order] = dot6(again[s], ortho[s])

    fresh_vs, pending = [], []
    for s in range(2):
        basis = ortho[s]
        back = dot3(basis, full_us[s])
        fresh_v = dot3(full_vs[s], back, NT) * (1.0 / root)
        fresh_u = basis.T * root
        fresh_vs.append(fresh_v)
        keep_u = cu[s]
        keep_v = cv[s]
        if panel == 0:
            keep_u = jnp.where(lanes < flags[2 + s], keep_u, 0.0)
            keep_v = jnp.where(lanes < flags[2 + s], keep_v, 0.0)
        elif s == 0:
            keep_v = jnp.where(flags[8] == 1, low.T, keep_v)
            keep_u = jnp.where(flags[9] == 1, 0.0, keep_u)
            keep_v = jnp.where(flags[9] == 1, 0.0, keep_v)
        chosen = flags[6 + s] == 1
        new_u = jnp.where(chosen, fresh_u, keep_u)
        new_v = jnp.where(chosen, fresh_v, keep_v)
        nu[s] = new_u
        nv[s] = new_v
        stores = [
            pltpu.make_async_copy(nu.at[s], to_u.at[s], sems.at[4 + 2 * s]),
            pltpu.make_async_copy(nv.at[s], to_v.at[s], sems.at[5 + 2 * s]),
        ]
        for store in stores:
            store.start()
        pending += stores
    if panel == 0:
        values = jnp.concatenate([ortho[0, :order], ortho[1, :order]], axis=0) * root
        for factors in parts[::-1]:
            values = values + dot3(values, factors, NT)
        values = values * start
        moved[:width] = extra[:width]
        moved[width:2 * width] = corner[0].T
        moved[2 * width:] = corner[1].T
        middle = flags[10] == 1
        fresh_t = fresh_vs[0].T[:order]
        pack[0] = ortho[0, :order] * root
        pack[1] = fresh_t
        out_z[0] = jnp.where(middle, moved[:order], values[:order])
        out_z[1] = values[order:]
        out_z[2] = moved[2 * order:3 * order]
        out_v[0] = jnp.where(middle, moved[order:2 * order], fresh_t)
        out_v[1] = fresh_vs[1].T[:order]
        out_v[2] = moved[3 * order:]
    for store in pending:
        store.wait()


def call(kernel, shapes, flags, *values, scratch=(), loads=0, stores=0):
    vmem, far = pl.BlockSpec(memory_space=pltpu.VMEM), pl.BlockSpec(memory_space=pltpu.HBM)
    shapes = tuple(jax.ShapeDtypeStruct(shape, F32) for shape in shapes)
    out = pl.pallas_call(
        kernel,
        out_shape=shapes,
        in_specs=[pl.BlockSpec(memory_space=pltpu.SMEM)] + [far] * loads + [vmem] * (len(values) - loads),
        out_specs=(far,) * stores + (vmem,) * (len(shapes) - stores),
        scratch_shapes=list(scratch),
        compiler_params=pltpu.CompilerParams(vmem_limit_bytes=24 * 1024 * 1024),
    )(flags, *values)
    return out if len(out) > 1 else out[0]


Z_COUNT = 4
X_COUNT = 4
COLS = 4


def row_of(z, x, core):
    return (z * X_COUNT + x) * 2 + core


def fan_out(value, axis, pair_sets):
    total = None
    for pairs in pair_sets:
        moved = lax.ppermute(value, axis, pairs)
        total = moved if total is None else total + moved
    return total


def share_planes(mine, row, before, beside):
    core = row % 2
    x = (row // 2) % X_COUNT
    z = row // (2 * X_COUNT)
    first = fan_out(
        mine,
        "row",
        [[(row_of(0, 0, 0), row_of(k, 0, 0)), (row_of(0, 0, 1), row_of(0, k, 1))] for k in (1, 3, 2)],
    )
    held, before = lax.optimization_barrier((jnp.where(row < 2, mine, first), before))
    second = fan_out(
        held,
        "row",
        [
            [(row_of(z, 0, 0), row_of(z, k, 0)) for z in range(Z_COUNT)]
            + [(row_of(0, x, 1), row_of(k, x, 1)) for x in range(X_COUNT)]
            for k in (1, 3, 2)
        ],
    )
    holder = jnp.where(core == 0, x, z) == 0
    final, beside = lax.optimization_barrier((jnp.where(holder, held, second), beside))
    other = lax.ppermute(final, "row", [(r, r ^ 1) for r in range(2 * X_COUNT * Z_COUNT)])
    return final, other, before, beside


def share_row(value, root, col, lowest):
    right, left, far = (root + 1) % COLS, (root + 3) % COLS, (root + 2) % COLS
    count = 2 * X_COUNT * Z_COUNT

    def pairs_of(pairs):
        return [(r * COLS + a, r * COLS + b) for r in range(lowest, count) for a, b in pairs]

    one = lax.ppermute(value, ("row", "col"), pairs_of([(root, right)]))
    held = jnp.where(col == root, value, one)

    def finish(held):
        two = lax.ppermute(held, ("row", "col"), pairs_of([(root, left), (right, far)]))
        return jnp.where((col == root) | (col == right), held, two)

    return held, finish


def share_pivots(value, roots):
    return fan_out(
        value,
        ("row", "col"),
        [[(r * COLS + c, r * COLS + (c + k) % COLS) for r, c in roots] for k in (1, 3, 2)],
    )


def body(factor_u, factor_v, near_field, sketch, tile_ranks):
    tile, width = factor_u.shape[4:]
    row = lax.axis_index("row")
    col = lax.axis_index("col")
    core = row % 2
    own_u = factor_u.reshape(2, tile, width)
    own_v = factor_v.reshape(2, tile, width)
    ranks = tile_ranks.reshape(3, -1, 2)
    own_ranks = lax.dynamic_slice_in_dim(ranks, row, 1, 1)[:, 0]
    order = (width - width // 4, width - width // 4 - (width - width // 4) // 4)

    def flags_of(panel):
        slots = jnp.arange(2) * 4 + col
        chosen = (row > panel) & (slots > panel)
        if panel == 0:
            chosen = chosen & jnp.logical_not((row == 1) & (slots == 1))
        lower = (row > col) & (col < 2)
        pivot = (row == col) & (col < 2)
        parts = [own_ranks[panel + 1], own_ranks[0], ranks[0, 0], chosen]
        parts += [lower[None], pivot[None], col[None], core[None]]
        return jnp.concatenate([part.astype(jnp.int32) for part in parts])

    flags = [flags_of(panel) for panel in range(2)]
    pair, payload = (2, tile, width), (2 * width, tile)
    packed = (3, order[0], tile)
    scratch = [
        [pltpu.VMEM((2, width, tile), F32), pltpu.VMEM((2, order[k], width), F32), pltpu.VMEM((4 * order[0], tile), F32)]
        + [pltpu.VMEM(shape, F32) for shape in (pair, pair, ((tile, tile), (2, tile, tile))[k], (tile, width), pair, pair)]
        + [pltpu.SemaphoreType.DMA((8,))]
        for k in range(2)
    ]

    with jax.named_scope("corner_share"):
        pack = jnp.stack([own_u[0], own_v[0]])
        got = share_pivots(pack, [(0, 0), (1, 1)])
        keep = jnp.arange(width, dtype=jnp.int32) < own_ranks[0, 0]
        kept = jnp.where(keep, jnp.stack([own_u[0], own_v[0]]), 0.0)
        near_lead, finish = share_row(kept, 0, col, 1)
        got, near_lead = lax.optimization_barrier((got, near_lead))
        corner = jnp.where(col == row, pack, got)
    with jax.named_scope("first_upper"):
        up_a, up_b = call(upper_kernel, (payload, payload), flags[0], near_field, corner, own_u, own_v)
    with jax.named_scope("upper_share"):
        crossed = lax.ppermute(up_a, "row", [(0, 1)])
        extra = call(wide_kernel, (payload,), flags[0], near_lead, crossed)
        mine, extra = lax.optimization_barrier((jnp.where(core == 0, up_b, crossed), extra))
        lead = finish(near_lead)
        got = share_pivots(extra, [(1, 1)])
        ours_0, theirs_0, lead, got = share_planes(mine, row, lead, got)
        extra = jnp.where(col == row, extra, got)
    with jax.named_scope("first_update"):
        cur_u, cur_v, pack, out_z, out_v = call(
            functools.partial(panel_kernel, order[0], 0),
            (pair, pair, (2, order[0], tile), packed, packed),
            flags[0], own_u, own_v, near_field, sketch, lead, ours_0, theirs_0, corner, extra,
            scratch=scratch[0], loads=4, stores=2,
        )
    with jax.named_scope("second_share"):
        near_lead, finish = share_row(pack, 1, col, 0)
        crossed = lax.ppermute(out_z, "row", [(1, 0)])
        ours, theirs, near_lead, _ = share_planes(jnp.where(core == 1, out_v, crossed), row, near_lead, row)
        lead = finish(near_lead)
    with jax.named_scope("second_update"):
        cur_u, cur_v = call(
            functools.partial(panel_kernel, order[1], 1),
            (pair, pair),
            flags[1], cur_u, cur_v, near_field, sketch, lead, ours, theirs, ours_0, theirs_0,
            scratch=scratch[1], loads=4, stores=2,
        )
    shape_out = factor_u.shape
    return cur_u.reshape(shape_out), cur_v.reshape(shape_out)


def solution(mesh):
    tiles = P(None, "row", None, "col", None, None)
    return jax.shard_map(
        body,
        mesh=mesh,
        in_specs=(tiles, tiles, P(), P(), P(None, None, None, None, "col")),
        out_specs=(tiles, tiles),
        check_vma=False,
    )
```

```python
import functools
import math
import jax
import jax.numpy as jnp
from jax import lax
from jax.experimental import pallas as pl
from jax.experimental.pallas import tpu as pltpu
from jax.sharding import PartitionSpec as P

F32 = jnp.float32
BF16 = jnp.bfloat16
NN = (((1,), (0,)), ((), ()))
NT = (((1,), (1,)), ((), ()))
TN = (((0,), (0,)), ((), ()))


def dot6(a, b, dims=NN):
    return lax.dot_general(a, b, dims, precision=lax.Precision.HIGHEST, preferred_element_type=F32)


def split(a):
    high = a.astype(BF16)
    return high, (a - high.astype(F32)).astype(BF16)


def dot1(a, b, dims=NN):
    return lax.dot_general(a, b, dims, preferred_element_type=F32)


def dot3(a, b, dims=NN):
    ah, al = a if isinstance(a, tuple) else split(a)
    bh, bl = b if isinstance(b, tuple) else split(b)
    return dot1(ah, bh, dims) + (dot1(ah, bl, dims) + dot1(al, bh, dims))


def iota(shape, axis):
    return lax.broadcasted_iota(jnp.int32, shape, axis)


def eliminate(grams, order, beside=()):
    count = len(grams)
    lane8 = iota((8, 128), 1)
    row8 = iota((8, 128), 0)
    blocks = [[g[8 * b:8 * b + 8, :] for b in range(order // 8)] for g in grams]
    done = [[] for _ in grams]
    steps = order // 8
    for step in range(steps):
        for task in beside[step * len(beside) // steps:(step + 1) * len(beside) // steps]:
            task()
        base = 8 * step
        panels, pivots_all = [], []
        for g in range(count):
            panel = blocks[g][step]
            cols = [jnp.broadcast_to(panel[:, base + c:base + c + 1], (8, 128)) for c in range(8)]
            inside = (lane8 >= base) & (lane8 < base + 8)
            work = jnp.where(inside, (lane8 - base == row8).astype(F32), panel)
            scale = jnp.zeros((8, 128), F32)
            for c in range(8):
                pivot = jnp.broadcast_to(cols[c][c:c + 1, :], (8, 128))
                inverse = 1.0 / pivot
                scale = jnp.where(row8 == c, inverse, scale)
                if c < 7:
                    factor = jnp.where(row8 > c, cols[c] * inverse, 0.0)
                    for d in range(c + 1, 8):
                        cols[d] = cols[d] - factor * jnp.broadcast_to(cols[d][c:c + 1, :], (8, 128))
                    work = work - factor * jnp.broadcast_to(work[c:c + 1, :], (8, 128))
            panels.append(work)
            pivots_all.append(scale)
        for g in range(count):
            work, scale = panels[g], pivots_all[g]
            done[g].append(work * jnp.sqrt(scale))
            if step + 1 < order // 8:
                update = dot6(work, work * scale, TN)
                inside = (lane8 >= base) & (lane8 < base + 8)
                for b in range(step + 1, order // 8):
                    blocks[g][b] = jnp.where(inside, 0.0, blocks[g][b]) - update[8 * b:8 * b + 8, :]
    outs = []
    for g in range(count):
        full = jnp.concatenate(done[g], axis=0)
        keep = iota((order, 128), 1) <= iota((order, 128), 0)
        outs.append(jnp.where(keep, full, 0.0))
    return outs


def wide_t(lead, z_t):
    weight = 1.0 / (8.0 * lead.shape[1])
    core_t = weight * dot3(z_t, lead[1])
    return core_t


def diagonal_inverse(far):
    eye = iota(far.shape, 0) == iota(far.shape, 1)
    return 1.0 / jnp.sum(jnp.where(eye, far, 0.0), axis=0, keepdims=True)


def series(pivot, start):
    eye = iota(pivot.shape, 0) == iota(pivot.shape, 1)
    rest = split(jnp.where(eye, 1.0, 0.0) - pivot * start)
    square = split(dot3(rest, rest))
    return rest, square, split(dot3(square, square))


def series_tasks(pivot, start, parts, values=None):
    eye = iota(pivot.shape, 0) == iota(pivot.shape, 1)
    parts.append(split(jnp.where(eye, 1.0, 0.0) - pivot * start))
    half = pivot.shape[0] // 2
    sums = {}

    def block(power, side, left, right):
        at = slice(side * half, side * half + half)
        high = parts[power]
        term = dot1(high[left], high[right][:, at])
        sums[side] = term if (left, right) == (0, 0) else sums[side] + term
        if side and (left, right) == (1, 0):
            parts.append(split(jnp.concatenate([sums[0], sums[1]], axis=1)))

    def apply(power):
        values[0] = values[0] + dot3(values[0], parts[power])

    tasks = []
    for power in range(3):
        if values is not None:
            tasks.append(functools.partial(apply, power))
        if power < 2:
            for side in range(2):
                for pair in ((0, 0), (0, 1), (1, 0)):
                    tasks.append(functools.partial(block, power, side, *pair))
    return tasks


def upper_kernel(flags, near, corner, own_u, own_v, out_a, out_b):
    tile, width = own_u.shape[1:]
    weight = 1.0 / (8.0 * tile)
    far = near[0]
    start = diagonal_inverse(far)
    parts = series(far + weight * dot3(corner[0], corner[1], NT), start)
    lanes = iota((tile, width), 1)
    values = jnp.concatenate([jnp.where(lanes < flags[2 + s], own_u[s], 0.0).T for s in range(2)], axis=0)
    for part in parts[::-1]:
        values = values + dot3(values, part, NT)
    values = values * start
    out_a[:width] = jnp.where(flags[10] == 0, corner[0].T, values[:width])
    out_a[width:] = own_v[0].T
    out_b[:width] = values[width:]
    out_b[width:] = own_v[1].T


def wide_kernel(flags, lead, crossed, out):
    width = lead.shape[2]
    out[:width] = dot3(wide_t(lead, crossed[:width]), lead[0], NT)
    out[width:] = crossed[width:]


def panel_kernel(order, panel, flags, far_u, far_v, far_near, far_sketch, lead, ours, theirs, *refs):
    if panel == 0:
        corner, extra, to_u, to_v, pack, out_z, out_v = refs[:7]
    else:
        ours_0, theirs_0, to_u, to_v = refs[:4]
    ortho, factor, moved, cu, cv, near, sketch, nu, nv, sems = refs[-10:]
    near_from = far_near.at[1] if panel == 0 else far_near
    loads = [
        pltpu.make_async_copy(far_v, cv, sems.at[0]),
        pltpu.make_async_copy(far_sketch.at[panel], sketch, sems.at[1]),
        pltpu.make_async_copy(far_u, cu, sems.at[2]),
        pltpu.make_async_copy(near_from, near, sems.at[3]),
    ]
    for load in loads:
        load.start()
    tile, width = cu.shape[1:]
    weight = 1.0 / (8.0 * tile)
    root = math.sqrt(tile)
    lanes = iota((tile, width), 1)
    spare = jnp.zeros((width - order, tile), F32)
    row_g = iota((order, width), 0)
    lane_g = iota((order, width), 1)
    eye = (row_g == lane_g).astype(F32)
    even = flags[11] == 0
    full_us, full_vs, bases, grams, units = [], [], [], [], []
    if panel == 1:
        part = ours.shape[1]
        rest = jnp.zeros((width - part, tile), F32)
        lead_u = jnp.concatenate([lead[0], rest], axis=0)
        lead_v = jnp.concatenate([lead[1], rest], axis=0)
    for load in loads:
        load.wait()
    test_t = sketch[...].T[:order]
    for s in range(2):
        own_u = cu[s]
        if panel == 0:
            own_u = jnp.where(lanes < flags[2 + s], own_u, 0.0)
            slot = jnp.where(even, theirs[...], ours[...]) if s == 0 else jnp.where(even, ours[...], theirs[...])
            up_v = slot[width:].T
            side = dot3(lead[0], wide_t(lead, slot[:width]), NT)
        else:
            z_t = jnp.concatenate([jnp.where(even, ours[s], theirs[s]), rest], axis=0)
            up_v = jnp.concatenate([jnp.where(even, theirs[s], ours[s]), rest], axis=0).T
            side = dot3(weight * dot3(z_t, lead_v, NT), lead_u).T
        full_u = jnp.concatenate([own_u, -side], axis=1)
        full_v = jnp.concatenate([cv[s], up_v], axis=1)
        projected = dot3(test_t, full_v)
        basis = dot3(projected, full_u, NT)
        basis = jnp.where(iota((order, tile), 0) < flags[s], basis, 0.0)
        basis = jnp.concatenate([basis, spare], axis=0)
        unit = jnp.where((row_g == lane_g) & (row_g >= flags[s]), 1.0, 0.0)
        grams.append(dot6(basis[:order], basis, NT) + unit)
        full_us.append(full_u)
        full_vs.append(full_v)
        bases.append(basis)
        units.append(unit)

    if panel == 0:
        far = near[...]
        start = diagonal_inverse(far)
        low_rank = dot3(corner[0], corner[1], NT) - dot3(extra[:width], extra[width:], TN)
        parts = []
        tasks = series_tasks(far + weight * low_rank, start, parts)
    else:
        left = flags[10] == 0
        slot = jnp.where(even, theirs_0[...], ours_0[...])
        moved[:part] = jnp.where(even, ours[0], theirs[0])
        moved[part:2 * part] = jnp.where(even, theirs[0], ours[0])
        moved[2 * part:3 * part] = jnp.where(even, ours[2], theirs[2])
        moved[3 * part:] = jnp.where(even, theirs[2], ours[2])
        far = jnp.where(left, near[0], near[1])
        start = diagonal_inverse(far)
        one_u = jnp.where(left, slot[:width], moved[width:2 * width])
        one_v = jnp.where(left, slot[width:], moved[2 * width:])
        two_u = jnp.where(left, 0.0, moved[:width])
        low_rank = dot3(one_u, one_v, TN) - dot3(two_u, slot[width:], TN)
        low = [cv[0].T * start]
        tasks = series_tasks(far + weight * low_rank, start, [], low)

    inverses = eliminate(grams, order, tasks)
    defect = jnp.zeros((), F32)
    for s in range(2):
        once = dot3(inverses[s], bases[s])
        ortho[s, :order] = once
        ortho[s, order:] = spare
        gram = dot3(once, jnp.concatenate([once, spare], axis=0), NT) + units[s]
        factor[s] = gram
        off = gram - eye
        defect = defect + jnp.where(flags[6 + s] == 1, jnp.sum(off * off), 0.0)
    near_unit = defect < 1e-6

    @pl.when(near_unit)
    def _():
        for s in range(2):
            off = factor[s] - eye
            half = jnp.where(lane_g < row_g, off, jnp.where(lane_g == row_g, 0.5 * off, 0.0))
            once = ortho[s]
            ortho[s, :order] = once[:order] - dot1(half.astype(BF16), once.astype(BF16))

    @pl.when(jnp.logical_not(near_unit))
    def _():
        again = eliminate([factor[0], factor[1]], order)
        for s in range(2):
            ortho[s, :order] = dot6(again[s], ortho[s])

    fresh_vs, pending = [], []
    for s in range(2):
        basis = ortho[s]
        back = dot3(basis, full_us[s])
        fresh_v = dot3(full_vs[s], back, NT) * (1.0 / root)
        fresh_u = basis.T * root
        fresh_vs.append(fresh_v)
        keep_u = cu[s]
        keep_v = cv[s]
        if panel == 0:
            keep_u = jnp.where(lanes < flags[2 + s], keep_u, 0.0)
            keep_v = jnp.where(lanes < flags[2 + s], keep_v, 0.0)
        elif s == 0:
            keep_v = jnp.where(flags[8] == 1, low[0].T, keep_v)
            keep_u = jnp.where(flags[9] == 1, 0.0, keep_u)
            keep_v = jnp.where(flags[9] == 1, 0.0, keep_v)
        chosen = flags[6 + s] == 1
        new_u = jnp.where(chosen, fresh_u, keep_u)
        new_v = jnp.where(chosen, fresh_v, keep_v)
        nu[s] = new_u
        nv[s] = new_v
        stores = [
            pltpu.make_async_copy(nu.at[s], to_u.at[s], sems.at[4 + 2 * s]),
            pltpu.make_async_copy(nv.at[s], to_v.at[s], sems.at[5 + 2 * s]),
        ]
        for store in stores:
            store.start()
        pending += stores
    if panel == 0:
        values = jnp.concatenate([ortho[0, :order], ortho[1, :order]], axis=0) * root
        for factors in parts[::-1]:
            values = values + dot3(values, factors, NT)
        values = values * start
        moved[:width] = extra[:width]
        moved[width:2 * width] = corner[0].T
        moved[2 * width:] = corner[1].T
        middle = flags[10] == 1
        fresh_t = fresh_vs[0].T[:order]
        pack[0] = ortho[0, :order] * root
        pack[1] = fresh_t
        out_z[0] = jnp.where(middle, moved[:order], values[:order])
        out_z[1] = values[order:]
        out_z[2] = moved[2 * order:3 * order]
        out_v[0] = jnp.where(middle, moved[order:2 * order], fresh_t)
        out_v[1] = fresh_vs[1].T[:order]
        out_v[2] = moved[3 * order:]
    for store in pending:
        store.wait()


def pack_kernel(flags, own_u, own_v, out, sems):
    loads = [
        pltpu.make_async_copy(own_u.at[0], out.at[0], sems.at[0]),
        pltpu.make_async_copy(own_v.at[0], out.at[1], sems.at[1]),
    ]
    for load in loads:
        load.start()
    for load in loads:
        load.wait()


def call(kernel, shapes, flags, *values, scratch=(), loads=0, stores=0):
    vmem, far = pl.BlockSpec(memory_space=pltpu.VMEM), pl.BlockSpec(memory_space=pltpu.HBM)
    shapes = tuple(jax.ShapeDtypeStruct(shape, F32) for shape in shapes)
    out = pl.pallas_call(
        kernel,
        out_shape=shapes,
        in_specs=[pl.BlockSpec(memory_space=pltpu.SMEM)] + [far] * loads + [vmem] * (len(values) - loads),
        out_specs=(far,) * stores + (vmem,) * (len(shapes) - stores),
        scratch_shapes=list(scratch),
        compiler_params=pltpu.CompilerParams(vmem_limit_bytes=24 * 1024 * 1024),
    )(flags, *values)
    return out if len(out) > 1 else out[0]


Z_COUNT = 4
X_COUNT = 4
COLS = 4


def row_of(z, x, core):
    return (z * X_COUNT + x) * 2 + core


def fan_out(value, axis, pair_sets):
    total = None
    for pairs in pair_sets:
        moved = lax.ppermute(value, axis, pairs)
        total = moved if total is None else total + moved
    return total


def share_planes(mine, row, before, beside):
    core = row % 2
    x = (row // 2) % X_COUNT
    z = row // (2 * X_COUNT)
    first = fan_out(
        mine,
        "row",
        [[(row_of(0, 0, 0), row_of(k, 0, 0)), (row_of(0, 0, 1), row_of(0, k, 1))] for k in (1, 3, 2)],
    )
    held, before = lax.optimization_barrier((jnp.where(row < 2, mine, first), before))
    second = fan_out(
        held,
        "row",
        [
            [(row_of(z, 0, 0), row_of(z, k, 0)) for z in range(Z_COUNT)]
            + [(row_of(0, x, 1), row_of(k, x, 1)) for x in range(X_COUNT)]
            for k in (1, 3, 2)
        ],
    )
    holder = jnp.where(core == 0, x, z) == 0
    final, beside = lax.optimization_barrier((jnp.where(holder, held, second), beside))
    other = lax.ppermute(final, "row", [(r, r ^ 1) for r in range(2 * X_COUNT * Z_COUNT)])
    return final, other, before, beside


def share_row(value, root, col, lowest):
    right, left, far = (root + 1) % COLS, (root + 3) % COLS, (root + 2) % COLS
    count = 2 * X_COUNT * Z_COUNT

    def pairs_of(pairs):
        return [(r * COLS + a, r * COLS + b) for r in range(lowest, count) for a, b in pairs]

    one = lax.ppermute(value, ("row", "col"), pairs_of([(root, right)]))
    held = jnp.where(col == root, value, one)

    def finish(held):
        two = lax.ppermute(held, ("row", "col"), pairs_of([(root, left), (right, far)]))
        return jnp.where((col == root) | (col == right), held, two)

    return held, finish


def share_pivots(value, roots):
    shares = [
        lax.ppermute(value, ("row", "col"), [(r * COLS + c, r * COLS + (c + k) % COLS) for r, c in roots])
        for k in (1, 3, 2)
    ]
    return shares[0], shares[1] + shares[2]


def body(factor_u, factor_v, near_field, sketch, tile_ranks):
    tile, width = factor_u.shape[4:]
    row = lax.axis_index("row")
    col = lax.axis_index("col")
    core = row % 2
    own_u = factor_u.reshape(2, tile, width)
    own_v = factor_v.reshape(2, tile, width)
    ranks = tile_ranks.reshape(3, -1, 2)
    own_ranks = lax.dynamic_slice_in_dim(ranks, row, 1, 1)[:, 0]
    order = (width - width // 4, width - width // 4 - (width - width // 4) // 4)

    def flags_of(panel):
        slots = jnp.arange(2) * 4 + col
        chosen = (row > panel) & (slots > panel)
        if panel == 0:
            chosen = chosen & jnp.logical_not((row == 1) & (slots == 1))
        lower = (row > col) & (col < 2)
        pivot = (row == col) & (col < 2)
        parts = [own_ranks[panel + 1], own_ranks[0], ranks[0, 0], chosen]
        parts += [lower[None], pivot[None], col[None], core[None]]
        return jnp.concatenate([part.astype(jnp.int32) for part in parts])

    flags = [flags_of(panel) for panel in range(2)]
    pair, payload = (2, tile, width), (2 * width, tile)
    packed = (3, order[0], tile)
    scratch = [
        [pltpu.VMEM((2, width, tile), F32), pltpu.VMEM((2, order[k], width), F32), pltpu.VMEM((4 * order[0], tile), F32)]
        + [pltpu.VMEM(shape, F32) for shape in (pair, pair, ((tile, tile), (2, tile, tile))[k], (tile, width), pair, pair)]
        + [pltpu.SemaphoreType.DMA((8,))]
        for k in range(2)
    ]

    with jax.named_scope("corner_share"):
        pack = call(
            pack_kernel, (pair,), col[None].astype(jnp.int32), own_u, own_v,
            scratch=[pltpu.SemaphoreType.DMA((2,))], loads=2,
        )
        near, others = share_pivots(pack, [(0, 0), (1, 1)])
        keep = jnp.arange(width, dtype=jnp.int32) < own_ranks[0, 0]
        kept, near = lax.optimization_barrier((pack, near))
        near_lead, finish = share_row(jnp.where(keep, kept, 0.0), 0, col, 1)
        got = near + others
        corner = jnp.where(col == row, pack, got)
    with jax.named_scope("first_upper"):
        up_a, up_b = call(upper_kernel, (payload, payload), flags[0], near_field, corner, own_u, own_v)
    with jax.named_scope("upper_share"):
        crossed = lax.ppermute(up_a, "row", [(0, 1)])
        extra = call(wide_kernel, (payload,), flags[0], near_lead, crossed)
        mine, extra = lax.optimization_barrier((jnp.where(core == 0, up_b, crossed), extra))
        lead = finish(near_lead)
        got = sum(share_pivots(extra, [(1, 1)]))
        ours_0, theirs_0, lead, got = share_planes(mine, row, lead, got)
        extra = jnp.where(col == row, extra, got)
    with jax.named_scope("first_update"):
        cur_u, cur_v, pack, out_z, out_v = call(
            functools.partial(panel_kernel, order[0], 0),
            (pair, pair, (2, order[0], tile), packed, packed),
            flags[0], own_u, own_v, near_field, sketch, lead, ours_0, theirs_0, corner, extra,
            scratch=scratch[0], loads=4, stores=2,
        )
    with jax.named_scope("second_share"):
        near_lead, finish = share_row(pack, 1, col, 0)
        crossed = lax.ppermute(out_z, "row", [(1, 0)])
        ours, theirs, near_lead, _ = share_planes(jnp.where(core == 1, out_v, crossed), row, near_lead, row)
        lead = finish(near_lead)
    with jax.named_scope("second_update"):
        cur_u, cur_v = call(
            functools.partial(panel_kernel, order[1], 1),
            (pair, pair),
            flags[1], cur_u, cur_v, near_field, sketch, lead, ours, theirs, ours_0, theirs_0,
            scratch=scratch[1], loads=4, stores=2,
        )
    shape_out = factor_u.shape
    return cur_u.reshape(shape_out), cur_v.reshape(shape_out)


def solution(mesh):
    tiles = P(None, "row", None, "col", None, None)
    return jax.shard_map(
        body,
        mesh=mesh,
        in_specs=(tiles, tiles, P(), P(), P(None, None, None, None, "col")),
        out_specs=(tiles, tiles),
        check_vma=False,
    )
```

```python
import functools
import math
import jax
import jax.numpy as jnp
from jax import lax
from jax.experimental import pallas as pl
from jax.experimental.pallas import tpu as pltpu
from jax.sharding import PartitionSpec as P

F32 = jnp.float32
BF16 = jnp.bfloat16
NN = (((1,), (0,)), ((), ()))
NT = (((1,), (1,)), ((), ()))
TN = (((0,), (0,)), ((), ()))


def dot6(a, b, dims=NN):
    return lax.dot_general(a, b, dims, precision=lax.Precision.HIGHEST, preferred_element_type=F32)


def split(a):
    high = a.astype(BF16)
    return high, (a - high.astype(F32)).astype(BF16)


def dot1(a, b, dims=NN):
    return lax.dot_general(a, b, dims, preferred_element_type=F32)


def dot3(a, b, dims=NN):
    ah, al = a if isinstance(a, tuple) else split(a)
    bh, bl = b if isinstance(b, tuple) else split(b)
    return dot1(ah, bh, dims) + (dot1(ah, bl, dims) + dot1(al, bh, dims))


def iota(shape, axis):
    return lax.broadcasted_iota(jnp.int32, shape, axis)


def eliminate(grams, order, beside=()):
    count = len(grams)
    lane8 = iota((8, 128), 1)
    row8 = iota((8, 128), 0)
    blocks = [[g[8 * b:8 * b + 8, :] for b in range(order // 8)] for g in grams]
    done = [[] for _ in grams]
    steps = order // 8
    for step in range(steps):
        for task in beside[step * len(beside) // steps:(step + 1) * len(beside) // steps]:
            task()
        base = 8 * step
        panels, pivots_all = [], []
        for g in range(count):
            panel = blocks[g][step]
            cols = [jnp.broadcast_to(panel[:, base + c:base + c + 1], (8, 128)) for c in range(8)]
            inside = (lane8 >= base) & (lane8 < base + 8)
            work = jnp.where(inside, (lane8 - base == row8).astype(F32), panel)
            scale = jnp.zeros((8, 128), F32)
            for c in range(8):
                pivot = jnp.broadcast_to(cols[c][c:c + 1, :], (8, 128))
                inverse = 1.0 / pivot
                scale = jnp.where(row8 == c, inverse, scale)
                if c < 7:
                    factor = jnp.where(row8 > c, cols[c] * inverse, 0.0)
                    for d in range(c + 1, 8):
                        cols[d] = cols[d] - factor * jnp.broadcast_to(cols[d][c:c + 1, :], (8, 128))
                    work = work - factor * jnp.broadcast_to(work[c:c + 1, :], (8, 128))
            panels.append(work)
            pivots_all.append(scale)
        for g in range(count):
            work, scale = panels[g], pivots_all[g]
            done[g].append(work * jnp.sqrt(scale))
            if step + 1 < order // 8:
                update = dot6(work, work * scale, TN)
                inside = (lane8 >= base) & (lane8 < base + 8)
                for b in range(step + 1, order // 8):
                    blocks[g][b] = jnp.where(inside, 0.0, blocks[g][b]) - update[8 * b:8 * b + 8, :]
    outs = []
    for g in range(count):
        full = jnp.concatenate(done[g], axis=0)
        keep = iota((order, 128), 1) <= iota((order, 128), 0)
        outs.append(jnp.where(keep, full, 0.0))
    return outs


def wide_t(lead, z_t):
    weight = 1.0 / (8.0 * lead.shape[1])
    core_t = weight * dot3(z_t, lead[1])
    return core_t


def diagonal_inverse(far):
    eye = iota(far.shape, 0) == iota(far.shape, 1)
    return 1.0 / jnp.sum(jnp.where(eye, far, 0.0), axis=0, keepdims=True)


def series(pivot, start):
    eye = iota(pivot.shape, 0) == iota(pivot.shape, 1)
    rest = split(jnp.where(eye, 1.0, 0.0) - pivot * start)
    square = split(dot3(rest, rest))
    return rest, square, split(dot3(square, square))


def series_tasks(pivot, start, parts, values=None):
    eye = iota(pivot.shape, 0) == iota(pivot.shape, 1)
    parts.append(split(jnp.where(eye, 1.0, 0.0) - pivot * start))
    half = pivot.shape[0] // 2
    sums = {}

    def block(power, side, left, right):
        at = slice(side * half, side * half + half)
        high = parts[power]
        term = dot1(high[left], high[right][:, at])
        sums[side] = term if (left, right) == (0, 0) else sums[side] + term
        if side and (left, right) == (1, 0):
            parts.append(split(jnp.concatenate([sums[0], sums[1]], axis=1)))

    def apply(power):
        values[0] = values[0] + dot3(values[0], parts[power])

    tasks = []
    for power in range(3):
        if values is not None:
            tasks.append(functools.partial(apply, power))
        if power < 2:
            for side in range(2):
                for pair in ((0, 0), (0, 1), (1, 0)):
                    tasks.append(functools.partial(block, power, side, *pair))
    return tasks


def upper_kernel(flags, near, corner, own_u, own_v, out_a, out_b):
    tile, width = own_u.shape[1:]
    weight = 1.0 / (8.0 * tile)
    far = near[0]
    start = diagonal_inverse(far)
    parts = series(far + weight * dot3(corner[0], corner[1], NT), start)
    lanes = iota((tile, width), 1)
    values = jnp.concatenate([jnp.where(lanes < flags[2 + s], own_u[s], 0.0).T for s in range(2)], axis=0)
    for part in parts[::-1]:
        values = values + dot3(values, part, NT)
    values = values * start
    out_a[:width] = jnp.where(flags[10] == 0, corner[0].T, values[:width])
    out_a[width:] = own_v[0].T
    out_b[:width] = values[width:]
    out_b[width:] = own_v[1].T


def wide_kernel(flags, lead, crossed, out):
    width = lead.shape[2]
    out[:width] = dot3(wide_t(lead, crossed[:width]), lead[0], NT)
    out[width:] = crossed[width:]


def panel_kernel(order, panel, flags, far_u, far_v, far_near, far_sketch, lead, ours, theirs, *refs):
    if panel == 0:
        corner, extra, to_u, to_v, pack, out_z, out_v = refs[:7]
    else:
        ours_0, theirs_0, to_u, to_v = refs[:4]
    ortho, factor, moved, cu, cv, near, sketch, nu, nv, sems = refs[-10:]
    near_from = far_near.at[1] if panel == 0 else far_near
    loads = [
        pltpu.make_async_copy(far_v, cv, sems.at[0]),
        pltpu.make_async_copy(far_sketch.at[panel], sketch, sems.at[1]),
        pltpu.make_async_copy(far_u, cu, sems.at[2]),
        pltpu.make_async_copy(near_from, near, sems.at[3]),
    ]
    for load in loads:
        load.start()
    tile, width = cu.shape[1:]
    weight = 1.0 / (8.0 * tile)
    root = math.sqrt(tile)
    lanes = iota((tile, width), 1)
    spare = jnp.zeros((width - order, tile), F32)
    row_g = iota((order, width), 0)
    lane_g = iota((order, width), 1)
    eye = (row_g == lane_g).astype(F32)
    even = flags[11] == 0
    full_us, full_vs, bases, grams, units = [], [], [], [], []
    if panel == 1:
        part = ours.shape[1]
        rest = jnp.zeros((width - part, tile), F32)
        lead_u = jnp.concatenate([lead[0], rest], axis=0)
        lead_v = jnp.concatenate([lead[1], rest], axis=0)
    for load in loads:
        load.wait()
    test_t = sketch[...].T[:order]
    for s in range(2):
        own_u = cu[s]
        if panel == 0:
            own_u = jnp.where(lanes < flags[2 + s], own_u, 0.0)
            slot = jnp.where(even, theirs[...], ours[...]) if s == 0 else jnp.where(even, ours[...], theirs[...])
            up_v = slot[width:].T
            side = dot3(lead[0], wide_t(lead, slot[:width]), NT)
        else:
            z_t = jnp.concatenate([jnp.where(even, ours[s], theirs[s]), rest], axis=0)
            up_v = jnp.concatenate([jnp.where(even, theirs[s], ours[s]), rest], axis=0).T
            side = dot3(weight * dot3(z_t, lead_v, NT), lead_u).T
        full_u = jnp.concatenate([own_u, -side], axis=1)
        full_v = jnp.concatenate([cv[s], up_v], axis=1)
        projected = dot3(test_t, full_v)
        basis = dot3(projected, full_u, NT)
        basis = jnp.where(iota((order, tile), 0) < flags[s], basis, 0.0)
        basis = jnp.concatenate([basis, spare], axis=0)
        unit = jnp.where((row_g == lane_g) & (row_g >= flags[s]), 1.0, 0.0)
        grams.append(dot6(basis[:order], basis, NT) + unit)
        full_us.append(full_u)
        full_vs.append(full_v)
        bases.append(basis)
        units.append(unit)

    if panel == 0:
        far = near[...]
        start = diagonal_inverse(far)
        low_rank = dot3(corner[0], corner[1], NT) - dot3(extra[:width], extra[width:], TN)
        parts = []
        tasks = series_tasks(far + weight * low_rank, start, parts)
    else:
        left = flags[10] == 0
        slot = jnp.where(even, theirs_0[...], ours_0[...])
        moved[:part] = jnp.where(even, ours[0], theirs[0])
        moved[part:2 * part] = jnp.where(even, theirs[0], ours[0])
        moved[2 * part:3 * part] = jnp.where(even, ours[2], theirs[2])
        moved[3 * part:] = jnp.where(even, theirs[2], ours[2])
        far = jnp.where(left, near[0], near[1])
        start = diagonal_inverse(far)
        one_u = jnp.where(left, slot[:width], moved[width:2 * width])
        one_v = jnp.where(left, slot[width:], moved[2 * width:])
        two_u = jnp.where(left, 0.0, moved[:width])
        low_rank = dot3(one_u, one_v, TN) - dot3(two_u, slot[width:], TN)
        low = [cv[0].T * start]
        tasks = series_tasks(far + weight * low_rank, start, [], low)

    inverses = eliminate(grams, order, tasks)
    defect = jnp.zeros((), F32)
    for s in range(2):
        once = dot3(inverses[s], bases[s])
        ortho[s, :order] = once
        ortho[s, order:] = spare
        gram = dot3(once, jnp.concatenate([once, spare], axis=0), NT) + units[s]
        factor[s] = gram
        off = gram - eye
        defect = defect + jnp.where(flags[6 + s] == 1, jnp.sum(off * off), 0.0)
    near_unit = defect < 1e-6

    @pl.when(near_unit)
    def _():
        for s in range(2):
            off = factor[s] - eye
            half = jnp.where(lane_g < row_g, off, jnp.where(lane_g == row_g, 0.5 * off, 0.0))
            once = ortho[s]
            ortho[s, :order] = once[:order] - dot1(half.astype(BF16), once.astype(BF16))

    @pl.when(jnp.logical_not(near_unit))
    def _():
        again = eliminate([factor[0], factor[1]], order)
        for s in range(2):
            ortho[s, :order] = dot6(again[s], ortho[s])

    fresh_vs, pending = [], []
    for s in range(2):
        basis = ortho[s]
        back = dot3(basis, full_us[s])
        fresh_v = dot3(full_vs[s], back, NT) * (1.0 / root)
        fresh_u = basis.T * root
        fresh_vs.append(fresh_v)
        keep_u = cu[s]
        keep_v = cv[s]
        if panel == 0:
            keep_u = jnp.where(lanes < flags[2 + s], keep_u, 0.0)
            keep_v = jnp.where(lanes < flags[2 + s], keep_v, 0.0)
        elif s == 0:
            keep_v = jnp.where(flags[8] == 1, low[0].T, keep_v)
            keep_u = jnp.where(flags[9] == 1, 0.0, keep_u)
            keep_v = jnp.where(flags[9] == 1, 0.0, keep_v)
        chosen = flags[6 + s] == 1
        new_u = jnp.where(chosen, fresh_u, keep_u)
        new_v = jnp.where(chosen, fresh_v, keep_v)
        nu[s] = new_u
        nv[s] = new_v
        stores = [
            pltpu.make_async_copy(nu.at[s], to_u.at[s], sems.at[4 + 2 * s]),
            pltpu.make_async_copy(nv.at[s], to_v.at[s], sems.at[5 + 2 * s]),
        ]
        for store in stores:
            store.start()
        pending += stores
    if panel == 0:
        values = jnp.concatenate([ortho[0, :order], ortho[1, :order]], axis=0) * root
        for factors in parts[::-1]:
            values = values + dot3(values, factors, NT)
        values = values * start
        moved[:width] = extra[:width]
        moved[width:2 * width] = corner[0].T
        moved[2 * width:] = corner[1].T
        middle = flags[10] == 1
        fresh_t = fresh_vs[0].T[:order]
        pack[0] = ortho[0, :order] * root
        pack[1] = fresh_t
        out_z[0] = jnp.where(middle, moved[:order], values[:order])
        out_z[1] = values[order:]
        out_z[2] = moved[2 * order:3 * order]
        out_v[0] = jnp.where(middle, moved[order:2 * order], fresh_t)
        out_v[1] = fresh_vs[1].T[:order]
        out_v[2] = moved[3 * order:]
    for store in pending:
        store.wait()


def pack_kernel(flags, own_u, own_v, out, sems):
    loads = [
        pltpu.make_async_copy(own_u.at[0], out.at[0], sems.at[0]),
        pltpu.make_async_copy(own_v.at[0], out.at[1], sems.at[1]),
    ]
    for load in loads:
        load.start()
    for load in loads:
        load.wait()


def call(kernel, shapes, flags, *values, scratch=(), loads=0, stores=0):
    vmem, far = pl.BlockSpec(memory_space=pltpu.VMEM), pl.BlockSpec(memory_space=pltpu.HBM)
    spaces = [pltpu.HBM] * stores + [pltpu.VMEM] * (len(shapes) - stores)
    shapes = tuple(space(shape, F32) for space, shape in zip(spaces, shapes))
    values = [pltpu.with_memory_space_constraint(value, pltpu.HBM) for value in values[:loads]] + list(values[loads:])
    out = pl.pallas_call(
        kernel,
        out_shape=shapes,
        in_specs=[pl.BlockSpec(memory_space=pltpu.SMEM)] + [far] * loads + [vmem] * (len(values) - loads),
        out_specs=(far,) * stores + (vmem,) * (len(shapes) - stores),
        scratch_shapes=list(scratch),
        compiler_params=pltpu.CompilerParams(vmem_limit_bytes=24 * 1024 * 1024),
    )(flags, *values)
    return out if len(out) > 1 else out[0]


Z_COUNT = 4
X_COUNT = 4
COLS = 4


def row_of(z, x, core):
    return (z * X_COUNT + x) * 2 + core


def fan_out(value, axis, pair_sets):
    total = None
    for pairs in pair_sets:
        moved = lax.ppermute(value, axis, pairs)
        total = moved if total is None else total + moved
    return total


def share_planes(mine, row, before, beside):
    core = row % 2
    x = (row // 2) % X_COUNT
    z = row // (2 * X_COUNT)
    first = fan_out(
        mine,
        "row",
        [[(row_of(0, 0, 0), row_of(k, 0, 0)), (row_of(0, 0, 1), row_of(0, k, 1))] for k in (1, 3, 2)],
    )
    held, before = lax.optimization_barrier((jnp.where(row < 2, mine, first), before))
    second = fan_out(
        held,
        "row",
        [
            [(row_of(z, 0, 0), row_of(z, k, 0)) for z in range(Z_COUNT)]
            + [(row_of(0, x, 1), row_of(k, x, 1)) for x in range(X_COUNT)]
            for k in (1, 3, 2)
        ],
    )
    holder = jnp.where(core == 0, x, z) == 0
    final, beside = lax.optimization_barrier((jnp.where(holder, held, second), beside))
    other = lax.ppermute(final, "row", [(r, r ^ 1) for r in range(2 * X_COUNT * Z_COUNT)])
    return final, other, before, beside


def share_row(value, root, col, lowest):
    right, left, far = (root + 1) % COLS, (root + 3) % COLS, (root + 2) % COLS
    count = 2 * X_COUNT * Z_COUNT

    def pairs_of(pairs):
        return [(r * COLS + a, r * COLS + b) for r in range(lowest, count) for a, b in pairs]

    one = lax.ppermute(value, ("row", "col"), pairs_of([(root, right)]))
    held = jnp.where(col == root, value, one)

    def finish(held):
        two = lax.ppermute(held, ("row", "col"), pairs_of([(root, left), (right, far)]))
        return jnp.where((col == root) | (col == right), held, two)

    return held, finish


def share_pivots(value, roots):
    shares = [
        lax.ppermute(value, ("row", "col"), [(r * COLS + c, r * COLS + (c + k) % COLS) for r, c in roots])
        for k in (1, 3, 2)
    ]
    return shares[0], shares[1] + shares[2]


def body(factor_u, factor_v, near_field, sketch, tile_ranks):
    tile, width = factor_u.shape[4:]
    row = lax.axis_index("row")
    col = lax.axis_index("col")
    core = row % 2
    own_u = factor_u.reshape(2, tile, width)
    own_v = factor_v.reshape(2, tile, width)
    ranks = tile_ranks.reshape(3, -1, 2)
    own_ranks = lax.dynamic_slice_in_dim(ranks, row, 1, 1)[:, 0]
    order = (width - width // 4, width - width // 4 - (width - width // 4) // 4)

    def flags_of(panel):
        slots = jnp.arange(2) * 4 + col
        chosen = (row > panel) & (slots > panel)
        if panel == 0:
            chosen = chosen & jnp.logical_not((row == 1) & (slots == 1))
        lower = (row > col) & (col < 2)
        pivot = (row == col) & (col < 2)
        parts = [own_ranks[panel + 1], own_ranks[0], ranks[0, 0], chosen]
        parts += [lower[None], pivot[None], col[None], core[None]]
        return jnp.concatenate([part.astype(jnp.int32) for part in parts])

    flags = [flags_of(panel) for panel in range(2)]
    pair, payload = (2, tile, width), (2 * width, tile)
    packed = (3, order[0], tile)
    scratch = [
        [pltpu.VMEM((2, width, tile), F32), pltpu.VMEM((2, order[k], width), F32), pltpu.VMEM((4 * order[0], tile), F32)]
        + [pltpu.VMEM(shape, F32) for shape in (pair, pair, ((tile, tile), (2, tile, tile))[k], (tile, width), pair, pair)]
        + [pltpu.SemaphoreType.DMA((8,))]
        for k in range(2)
    ]

    with jax.named_scope("corner_share"):
        pack = call(
            pack_kernel, (pair,), col[None].astype(jnp.int32), own_u, own_v,
            scratch=[pltpu.SemaphoreType.DMA((2,))], loads=2,
        )
        near, others = share_pivots(pack, [(0, 0), (1, 1)])
        keep = jnp.arange(width, dtype=jnp.int32) < own_ranks[0, 0]
        kept, near = lax.optimization_barrier((pack, near))
        near_lead, finish = share_row(jnp.where(keep, kept, 0.0), 0, col, 1)
        got = near + others
        corner = jnp.where(col == row, pack, got)
    with jax.named_scope("first_upper"):
        up_a, up_b = call(upper_kernel, (payload, payload), flags[0], near_field, corner, own_u, own_v)
    with jax.named_scope("upper_share"):
        crossed = lax.ppermute(up_a, "row", [(0, 1)])
        extra = call(wide_kernel, (payload,), flags[0], near_lead, crossed)
        mine, extra = lax.optimization_barrier((jnp.where(core == 0, up_b, crossed), extra))
        got = sum(share_pivots(extra, [(1, 1)]))
        ours_0, theirs_0, near_lead, got = share_planes(mine, row, near_lead, got)
        lead = finish(near_lead)
        extra = jnp.where(col == row, extra, got)
    with jax.named_scope("first_update"):
        cur_u, cur_v, pack, out_z, out_v = call(
            functools.partial(panel_kernel, order[0], 0),
            (pair, pair, (2, order[0], tile), packed, packed),
            flags[0], own_u, own_v, near_field, sketch, lead, ours_0, theirs_0, corner, extra,
            scratch=scratch[0], loads=4, stores=2,
        )
    with jax.named_scope("second_share"):
        near_lead, finish = share_row(pack, 1, col, 0)
        crossed = lax.ppermute(out_z, "row", [(1, 0)])
        ours, theirs, near_lead, _ = share_planes(jnp.where(core == 1, out_v, crossed), row, near_lead, row)
        lead = finish(near_lead)
    with jax.named_scope("second_update"):
        cur_u, cur_v = call(
            functools.partial(panel_kernel, order[1], 1),
            (pair, pair),
            flags[1], cur_u, cur_v, near_field, sketch, lead, ours, theirs, ours_0, theirs_0,
            scratch=scratch[1], loads=4, stores=2,
        )
    shape_out = factor_u.shape
    return cur_u.reshape(shape_out), cur_v.reshape(shape_out)


def solution(mesh):
    tiles = P(None, "row", None, "col", None, None)
    return jax.shard_map(
        body,
        mesh=mesh,
        in_specs=(tiles, tiles, P(), P(), P(None, None, None, None, "col")),
        out_specs=(tiles, tiles),
        check_vma=False,
    )
```

```python
import functools
import math
import jax
import jax.numpy as jnp
from jax import lax
from jax.experimental import pallas as pl
from jax.experimental.pallas import tpu as pltpu
from jax.sharding import PartitionSpec as P

F32 = jnp.float32
BF16 = jnp.bfloat16
NN = (((1,), (0,)), ((), ()))
NT = (((1,), (1,)), ((), ()))
TN = (((0,), (0,)), ((), ()))


def dot6(a, b, dims=NN):
    return lax.dot_general(a, b, dims, precision=lax.Precision.HIGHEST, preferred_element_type=F32)


def split(a):
    high = a.astype(BF16)
    return high, (a - high.astype(F32)).astype(BF16)


def dot1(a, b, dims=NN):
    return lax.dot_general(a, b, dims, preferred_element_type=F32)


def dot3(a, b, dims=NN):
    ah, al = a if isinstance(a, tuple) else split(a)
    bh, bl = b if isinstance(b, tuple) else split(b)
    return dot1(ah, bh, dims) + (dot1(ah, bl, dims) + dot1(al, bh, dims))


def iota(shape, axis):
    return lax.broadcasted_iota(jnp.int32, shape, axis)


def eliminate(grams, order, beside=()):
    count = len(grams)
    lane8 = iota((8, 128), 1)
    row8 = iota((8, 128), 0)
    blocks = [[g[8 * b:8 * b + 8, :] for b in range(order // 8)] for g in grams]
    done = [[] for _ in grams]
    steps = order // 8
    for step in range(steps):
        for task in beside[step * len(beside) // steps:(step + 1) * len(beside) // steps]:
            task()
        base = 8 * step
        panels, pivots_all = [], []
        for g in range(count):
            panel = blocks[g][step]
            cols = [jnp.broadcast_to(panel[:, base + c:base + c + 1], (8, 128)) for c in range(8)]
            inside = (lane8 >= base) & (lane8 < base + 8)
            work = jnp.where(inside, (lane8 - base == row8).astype(F32), panel)
            scale = jnp.zeros((8, 128), F32)
            for c in range(8):
                pivot = jnp.broadcast_to(cols[c][c:c + 1, :], (8, 128))
                inverse = 1.0 / pivot
                scale = jnp.where(row8 == c, inverse, scale)
                if c < 7:
                    factor = jnp.where(row8 > c, cols[c] * inverse, 0.0)
                    for d in range(c + 1, 8):
                        cols[d] = cols[d] - factor * jnp.broadcast_to(cols[d][c:c + 1, :], (8, 128))
                    work = work - factor * jnp.broadcast_to(work[c:c + 1, :], (8, 128))
            panels.append(work)
            pivots_all.append(scale)
        for g in range(count):
            work, scale = panels[g], pivots_all[g]
            done[g].append(work * jnp.sqrt(scale))
            if step + 1 < order // 8:
                update = dot6(work, work * scale, TN)
                inside = (lane8 >= base) & (lane8 < base + 8)
                for b in range(step + 1, order // 8):
                    blocks[g][b] = jnp.where(inside, 0.0, blocks[g][b]) - update[8 * b:8 * b + 8, :]
    outs = []
    for g in range(count):
        full = jnp.concatenate(done[g], axis=0)
        keep = iota((order, 128), 1) <= iota((order, 128), 0)
        outs.append(jnp.where(keep, full, 0.0))
    return outs


def wide_t(lead, z_t):
    weight = 1.0 / (8.0 * lead.shape[1])
    core_t = weight * dot3(z_t, lead[1])
    return core_t


def diagonal_inverse(far):
    eye = iota(far.shape, 0) == iota(far.shape, 1)
    return 1.0 / jnp.sum(jnp.where(eye, far, 0.0), axis=0, keepdims=True)


def series(pivot, start):
    eye = iota(pivot.shape, 0) == iota(pivot.shape, 1)
    rest = split(jnp.where(eye, 1.0, 0.0) - pivot * start)
    square = split(dot3(rest, rest))
    return rest, square, split(dot3(square, square))


def series_tasks(pivot, start, parts, values=None):
    eye = iota(pivot.shape, 0) == iota(pivot.shape, 1)
    parts.append(split(jnp.where(eye, 1.0, 0.0) - pivot * start))
    half = pivot.shape[0] // 2
    sums = {}

    def block(power, side, left, right):
        at = slice(side * half, side * half + half)
        high = parts[power]
        term = dot1(high[left], high[right][:, at])
        sums[side] = term if (left, right) == (0, 0) else sums[side] + term
        if side and (left, right) == (1, 0):
            parts.append(split(jnp.concatenate([sums[0], sums[1]], axis=1)))

    def apply(power):
        values[0] = values[0] + dot3(values[0], parts[power])

    tasks = []
    for power in range(3):
        if values is not None:
            tasks.append(functools.partial(apply, power))
        if power < 2:
            for side in range(2):
                for pair in ((0, 0), (0, 1), (1, 0)):
                    tasks.append(functools.partial(block, power, side, *pair))
    return tasks


def upper_kernel(flags, near, corner, own_u, own_v, *outs):
    tile, width = own_u.shape[1:]
    weight = 1.0 / (8.0 * tile)
    far = near[0]
    start = diagonal_inverse(far)
    parts = series(far + weight * dot3(corner[0], corner[1], NT), start)
    lanes = iota((tile, width), 1)
    values = jnp.concatenate([jnp.where(lanes < flags[2 + s], own_u[s], 0.0).T for s in range(2)], axis=0)
    for part in parts[::-1]:
        values = values + dot3(values, part, NT)
    values = values * start
    outs[0][...] = jnp.where(flags[10] == 0, corner[0].T, values[:width])
    outs[1][...] = own_v[0].T
    outs[2][...] = values[width:]
    outs[3][...] = own_v[1].T


def wide_kernel(flags, lead, z_t, v_t, out):
    width = lead.shape[2]
    out[:width] = dot3(wide_t(lead, z_t[...]), lead[0], NT)
    out[width:] = v_t[...]


def panel_kernel(order, panel, flags, far_u, far_v, far_near, far_sketch, lead, *refs):
    ours, theirs, refs = refs[:2], refs[2:4], refs[4:]
    if panel == 0:
        corner, extra, to_u, to_v, pack = refs[:5]
        out_z, out_v = refs[5:7], refs[7:9]
    else:
        ours_0, theirs_0, to_u, to_v = refs[:2], refs[2:4], refs[4], refs[5]
    ortho, factor, moved, cu, cv, near, sketch, nu, nv, sems = refs[-10:]
    near_from = far_near.at[1] if panel == 0 else far_near
    loads = [
        pltpu.make_async_copy(far_v, cv, sems.at[0]),
        pltpu.make_async_copy(far_sketch.at[panel], sketch, sems.at[1]),
        pltpu.make_async_copy(far_u, cu, sems.at[2]),
        pltpu.make_async_copy(near_from, near, sems.at[3]),
    ]
    for load in loads:
        load.start()
    tile, width = cu.shape[1:]
    even = flags[11] == 0
    weight = 1.0 / (8.0 * tile)
    root = math.sqrt(tile)
    lanes = iota((tile, width), 1)
    spare = jnp.zeros((width - order, tile), F32)
    row_g = iota((order, width), 0)
    lane_g = iota((order, width), 1)
    eye = (row_g == lane_g).astype(F32)
    full_us, full_vs, bases, grams, units = [], [], [], [], []
    if panel == 1:
        part = 2 * ours[0].shape[0] // 3
        rest = jnp.zeros((width - part, tile), F32)
        lead_u = jnp.concatenate([lead[0], rest], axis=0)
        lead_v = jnp.concatenate([lead[1], rest], axis=0)
        cut = part // 2
        planes = []
        for one, two in ((ours, theirs), (theirs, ours)):
            head, tail = [jnp.where(even, one[at][...], two[at][...]) for at in range(2)]
            planes.append([head[:part], jnp.concatenate([head[part:], tail[:cut]], axis=0), tail[cut:]])
        z_rows, v_rows = planes
    for load in loads:
        load.wait()
    test_t = sketch[...].T[:order]
    for s in range(2):
        own_u = cu[s]
        if panel == 0:
            own_u = jnp.where(lanes < flags[2 + s], own_u, 0.0)
            one, two = (theirs, ours) if s == 0 else (ours, theirs)
            up_v = jnp.where(even, one[1][...], two[1][...]).T
            side = dot3(lead[0], wide_t(lead, jnp.where(even, one[0][...], two[0][...])), NT)
        else:
            z_t = jnp.concatenate([z_rows[s], rest], axis=0)
            up_v = jnp.concatenate([v_rows[s], rest], axis=0).T
            side = dot3(weight * dot3(z_t, lead_v, NT), lead_u).T
        full_u = jnp.concatenate([own_u, -side], axis=1)
        full_v = jnp.concatenate([cv[s], up_v], axis=1)
        projected = dot3(test_t, full_v)
        basis = dot3(projected, full_u, NT)
        basis = jnp.where(iota((order, tile), 0) < flags[s], basis, 0.0)
        basis = jnp.concatenate([basis, spare], axis=0)
        unit = jnp.where((row_g == lane_g) & (row_g >= flags[s]), 1.0, 0.0)
        grams.append(dot6(basis[:order], basis, NT) + unit)
        full_us.append(full_u)
        full_vs.append(full_v)
        bases.append(basis)
        units.append(unit)

    if panel == 0:
        far = near[...]
        start = diagonal_inverse(far)
        low_rank = dot3(corner[0], corner[1], NT) - dot3(extra[:width], extra[width:], TN)
        parts = []
        tasks = series_tasks(far + weight * low_rank, start, parts)
    else:
        left = flags[10] == 0
        first_u, first_v = [jnp.where(even, theirs_0[at][...], ours_0[at][...]) for at in range(2)]
        moved[:part] = z_rows[0]
        moved[part:2 * part] = v_rows[0]
        moved[2 * part:3 * part] = z_rows[2]
        moved[3 * part:] = v_rows[2]
        far = jnp.where(left, near[0], near[1])
        start = diagonal_inverse(far)
        one_u = jnp.where(left, first_u, moved[width:2 * width])
        one_v = jnp.where(left, first_v, moved[2 * width:])
        two_u = jnp.where(left, 0.0, moved[:width])
        low_rank = dot3(one_u, one_v, TN) - dot3(two_u, first_v, TN)
        low = [cv[0].T * start]
        tasks = series_tasks(far + weight * low_rank, start, [], low)

    inverses = eliminate(grams, order, tasks)
    defect = jnp.zeros((), F32)
    for s in range(2):
        once = dot3(inverses[s], bases[s])
        ortho[s, :order] = once
        ortho[s, order:] = spare
        gram = dot3(once, jnp.concatenate([once, spare], axis=0), NT) + units[s]
        factor[s] = gram
        off = gram - eye
        defect = defect + jnp.where(flags[6 + s] == 1, jnp.sum(off * off), 0.0)
    near_unit = defect < 1e-6

    @pl.when(near_unit)
    def _():
        for s in range(2):
            off = factor[s] - eye
            half = jnp.where(lane_g < row_g, off, jnp.where(lane_g == row_g, 0.5 * off, 0.0))
            once = ortho[s]
            ortho[s, :order] = once[:order] - dot1(half.astype(BF16), once.astype(BF16))

    @pl.when(jnp.logical_not(near_unit))
    def _():
        again = eliminate([factor[0], factor[1]], order)
        for s in range(2):
            ortho[s, :order] = dot6(again[s], ortho[s])

    fresh_vs, pending = [], []
    for s in range(2):
        basis = ortho[s]
        back = dot3(basis, full_us[s])
        fresh_v = dot3(full_vs[s], back, NT) * (1.0 / root)
        fresh_u = basis.T * root
        fresh_vs.append(fresh_v)
        keep_u = cu[s]
        keep_v = cv[s]
        if panel == 0:
            keep_u = jnp.where(lanes < flags[2 + s], keep_u, 0.0)
            keep_v = jnp.where(lanes < flags[2 + s], keep_v, 0.0)
        elif s == 0:
            keep_v = jnp.where(flags[8] == 1, low[0].T, keep_v)
            keep_u = jnp.where(flags[9] == 1, 0.0, keep_u)
            keep_v = jnp.where(flags[9] == 1, 0.0, keep_v)
        chosen = flags[6 + s] == 1
        new_u = jnp.where(chosen, fresh_u, keep_u)
        new_v = jnp.where(chosen, fresh_v, keep_v)
        nu[s] = new_u
        nv[s] = new_v
        stores = [
            pltpu.make_async_copy(nu.at[s], to_u.at[s], sems.at[4 + 2 * s]),
            pltpu.make_async_copy(nv.at[s], to_v.at[s], sems.at[5 + 2 * s]),
        ]
        for store in stores:
            store.start()
        pending += stores
    if panel == 0:
        values = jnp.concatenate([ortho[0, :order], ortho[1, :order]], axis=0) * root
        for factors in parts[::-1]:
            values = values + dot3(values, factors, NT)
        values = values * start
        moved[:width] = extra[:width]
        moved[width:2 * width] = corner[0].T
        moved[2 * width:] = corner[1].T
        middle = flags[10] == 1
        fresh_t = fresh_vs[0].T[:order]
        pack[0] = ortho[0, :order] * root
        pack[1] = fresh_t
        cut = order // 2
        z_rows = [jnp.where(middle, moved[:order], values[:order]), values[order:], moved[2 * order:3 * order]]
        v_rows = [jnp.where(middle, moved[order:2 * order], fresh_t), fresh_vs[1].T[:order], moved[3 * order:]]
        for (head, tail), rows in ((out_z, z_rows), (out_v, v_rows)):
            head[:order] = rows[0]
            head[order:] = rows[1][:cut]
            tail[:cut] = rows[1][cut:]
            tail[cut:] = rows[2]
    for store in pending:
        store.wait()


def pack_kernel(flags, own_u, own_v, out, sems):
    loads = [
        pltpu.make_async_copy(own_u.at[0], out.at[0], sems.at[0]),
        pltpu.make_async_copy(own_v.at[0], out.at[1], sems.at[1]),
    ]
    for load in loads:
        load.start()
    for load in loads:
        load.wait()


def call(kernel, shapes, flags, *values, scratch=(), loads=0, stores=0):
    vmem, far = pl.BlockSpec(memory_space=pltpu.VMEM), pl.BlockSpec(memory_space=pltpu.HBM)
    spaces = [pltpu.HBM] * stores + [pltpu.VMEM] * (len(shapes) - stores)
    shapes = tuple(space(shape, F32) for space, shape in zip(spaces, shapes))
    values = [pltpu.with_memory_space_constraint(value, pltpu.HBM) for value in values[:loads]] + list(values[loads:])
    out = pl.pallas_call(
        kernel,
        out_shape=shapes,
        in_specs=[pl.BlockSpec(memory_space=pltpu.SMEM)] + [far] * loads + [vmem] * (len(values) - loads),
        out_specs=(far,) * stores + (vmem,) * (len(shapes) - stores),
        scratch_shapes=list(scratch),
        compiler_params=pltpu.CompilerParams(vmem_limit_bytes=24 * 1024 * 1024),
    )(flags, *values)
    return out if len(out) > 1 else out[0]


Z_COUNT = 4
X_COUNT = 4
COLS = 4


def row_of(z, x, core):
    return (z * X_COUNT + x) * 2 + core


def fan_out(value, axis, pair_sets):
    total = None
    for pairs in pair_sets:
        moved = lax.ppermute(value, axis, pairs)
        total = moved if total is None else total + moved
    return total


def share_planes(pieces, row, before, beside):
    core = row % 2
    x = (row // 2) % X_COUNT
    z = row // (2 * X_COUNT)
    first_sets = [[(row_of(0, 0, 0), row_of(k, 0, 0)), (row_of(0, 0, 1), row_of(0, k, 1))] for k in (1, 3, 2)]
    second_sets = [
        [(row_of(z, 0, 0), row_of(z, k, 0)) for z in range(Z_COUNT)]
        + [(row_of(0, x, 1), row_of(k, x, 1)) for x in range(X_COUNT)]
        for k in (1, 3, 2)
    ]
    holder = jnp.where(core == 0, x, z) == 0
    ours, theirs = [], []
    for at, mine in enumerate(pieces):
        held = jnp.where(row < 2, mine, fan_out(mine, "row", first_sets))
        if at == 1:
            held, before = lax.optimization_barrier((held, before))
        final = jnp.where(holder, held, fan_out(held, "row", second_sets))
        if at == 1:
            final, beside = lax.optimization_barrier((final, beside))
        ours.append(final)
        theirs.append(lax.ppermute(final, "row", [(r, r ^ 1) for r in range(2 * X_COUNT * Z_COUNT)]))
    return ours, theirs, before, beside


def share_row(value, root, col, lowest):
    right, left, far = (root + 1) % COLS, (root + 3) % COLS, (root + 2) % COLS
    count = 2 * X_COUNT * Z_COUNT

    def pairs_of(pairs):
        return [(r * COLS + a, r * COLS + b) for r in range(lowest, count) for a, b in pairs]

    one = lax.ppermute(value, ("row", "col"), pairs_of([(root, right)]))
    held = jnp.where(col == root, value, one)

    def finish(held):
        two = lax.ppermute(held, ("row", "col"), pairs_of([(root, left), (right, far)]))
        return jnp.where((col == root) | (col == right), held, two)

    return held, finish


def share_pivots(value, roots):
    shares = [
        lax.ppermute(value, ("row", "col"), [(r * COLS + c, r * COLS + (c + k) % COLS) for r, c in roots])
        for k in (1, 3, 2)
    ]
    return shares[0], shares[1] + shares[2]


def body(factor_u, factor_v, near_field, sketch, tile_ranks):
    tile, width = factor_u.shape[4:]
    row = lax.axis_index("row")
    col = lax.axis_index("col")
    core = row % 2
    own_u = factor_u.reshape(2, tile, width)
    own_v = factor_v.reshape(2, tile, width)
    ranks = tile_ranks.reshape(3, -1, 2)
    own_ranks = lax.dynamic_slice_in_dim(ranks, row, 1, 1)[:, 0]
    order = (width - width // 4, width - width // 4 - (width - width // 4) // 4)

    def flags_of(panel):
        slots = jnp.arange(2) * 4 + col
        chosen = (row > panel) & (slots > panel)
        if panel == 0:
            chosen = chosen & jnp.logical_not((row == 1) & (slots == 1))
        lower = (row > col) & (col < 2)
        pivot = (row == col) & (col < 2)
        parts = [own_ranks[panel + 1], own_ranks[0], ranks[0, 0], chosen]
        parts += [lower[None], pivot[None], col[None], core[None]]
        return jnp.concatenate([part.astype(jnp.int32) for part in parts])

    flags = [flags_of(panel) for panel in range(2)]
    pair, payload = (2, tile, width), (2 * width, tile)
    packed = (3 * order[0] // 2, tile)
    scratch = [
        [pltpu.VMEM((2, width, tile), F32), pltpu.VMEM((2, order[k], width), F32), pltpu.VMEM((4 * order[0], tile), F32)]
        + [pltpu.VMEM(shape, F32) for shape in (pair, pair, ((tile, tile), (2, tile, tile))[k], (tile, width), pair, pair)]
        + [pltpu.SemaphoreType.DMA((8,))]
        for k in range(2)
    ]

    with jax.named_scope("corner_share"):
        pack = call(
            pack_kernel, (pair,), col[None].astype(jnp.int32), own_u, own_v,
            scratch=[pltpu.SemaphoreType.DMA((2,))], loads=2,
        )
        near, others = share_pivots(pack, [(0, 0), (1, 1)])
        keep = jnp.arange(width, dtype=jnp.int32) < own_ranks[0, 0]
        kept, near = lax.optimization_barrier((pack, near))
        near_lead, finish = share_row(jnp.where(keep, kept, 0.0), 0, col, 1)
        got = near + others
        corner = jnp.where(col == row, pack, got)
    with jax.named_scope("first_upper"):
        ups = call(upper_kernel, ((width, tile),) * 4, flags[0], near_field, corner, own_u, own_v)
    with jax.named_scope("upper_share"):
        *sent, near_lead = lax.optimization_barrier((*ups[:2], near_lead))
        crossed = [lax.ppermute(up, "row", [(0, 1)]) for up in sent]
        extra = call(wide_kernel, (payload,), flags[0], near_lead, *crossed)
        pieces = [jnp.where(core == 0, up, other) for up, other in zip(ups[2:], crossed)]
        *pieces, extra = lax.optimization_barrier((*pieces, extra))
        got = sum(share_pivots(extra, [(1, 1)]))
        ours_0, theirs_0, near_lead, got = share_planes(pieces, row, near_lead, got)
        lead = finish(near_lead)
        extra = jnp.where(col == row, extra, got)
    with jax.named_scope("first_update"):
        cur_u, cur_v, pack, *outs = call(
            functools.partial(panel_kernel, order[0], 0),
            (pair, pair, (2, order[0], tile), packed, packed, packed, packed),
            flags[0], own_u, own_v, near_field, sketch, lead, *ours_0, *theirs_0, corner, extra,
            scratch=scratch[0], loads=4, stores=2,
        )
    with jax.named_scope("second_share"):
        near_lead, finish = share_row(pack, 1, col, 0)
        crossed = [lax.ppermute(out, "row", [(1, 0)]) for out in outs[:2]]
        pieces = [jnp.where(core == 1, out, other) for out, other in zip(outs[2:], crossed)]
        ours, theirs, near_lead, _ = share_planes(pieces, row, near_lead, row)
        lead = finish(near_lead)
    with jax.named_scope("second_update"):
        cur_u, cur_v = call(
            functools.partial(panel_kernel, order[1], 1),
            (pair, pair),
            flags[1], cur_u, cur_v, near_field, sketch, lead, *ours, *theirs, *ours_0, *theirs_0,
            scratch=scratch[1], loads=4, stores=2,
        )
    shape_out = factor_u.shape
    return cur_u.reshape(shape_out), cur_v.reshape(shape_out)


def solution(mesh):
    tiles = P(None, "row", None, "col", None, None)
    return jax.shard_map(
        body,
        mesh=mesh,
        in_specs=(tiles, tiles, P(), P(), P(None, None, None, None, "col")),
        out_specs=(tiles, tiles),
        check_vma=False,
    )
```

```python
import functools
import math
import jax
import jax.numpy as jnp
from jax import lax
from jax.experimental import pallas as pl
from jax.experimental.pallas import tpu as pltpu
from jax.sharding import PartitionSpec as P

F32 = jnp.float32
BF16 = jnp.bfloat16
NN = (((1,), (0,)), ((), ()))
NT = (((1,), (1,)), ((), ()))
TN = (((0,), (0,)), ((), ()))


def dot6(a, b, dims=NN):
    return lax.dot_general(a, b, dims, precision=lax.Precision.HIGHEST, preferred_element_type=F32)


def split(a):
    high = a.astype(BF16)
    return high, (a - high.astype(F32)).astype(BF16)


def dot1(a, b, dims=NN):
    return lax.dot_general(a, b, dims, preferred_element_type=F32)


def dot3(a, b, dims=NN):
    ah, al = a if isinstance(a, tuple) else split(a)
    bh, bl = b if isinstance(b, tuple) else split(b)
    return dot1(ah, bh, dims) + (dot1(ah, bl, dims) + dot1(al, bh, dims))


def iota(shape, axis):
    return lax.broadcasted_iota(jnp.int32, shape, axis)


def eliminate(grams, order, beside=()):
    count = len(grams)
    lane8 = iota((8, 128), 1)
    row8 = iota((8, 128), 0)
    blocks = [[g[8 * b:8 * b + 8, :] for b in range(order // 8)] for g in grams]
    done = [[] for _ in grams]
    steps = order // 8
    for step in range(steps):
        for task in beside[step * len(beside) // steps:(step + 1) * len(beside) // steps]:
            task()
        base = 8 * step
        panels, pivots_all = [], []
        for g in range(count):
            panel = blocks[g][step]
            cols = [jnp.broadcast_to(panel[:, base + c:base + c + 1], (8, 128)) for c in range(8)]
            inside = (lane8 >= base) & (lane8 < base + 8)
            work = jnp.where(inside, (lane8 - base == row8).astype(F32), panel)
            scale = jnp.zeros((8, 128), F32)
            for c in range(8):
                pivot = jnp.broadcast_to(cols[c][c:c + 1, :], (8, 128))
                inverse = 1.0 / pivot
                scale = jnp.where(row8 == c, inverse, scale)
                if c < 7:
                    factor = jnp.where(row8 > c, cols[c] * inverse, 0.0)
                    for d in range(c + 1, 8):
                        cols[d] = cols[d] - factor * jnp.broadcast_to(cols[d][c:c + 1, :], (8, 128))
                    work = work - factor * jnp.broadcast_to(work[c:c + 1, :], (8, 128))
            panels.append(work)
            pivots_all.append(scale)
        for g in range(count):
            work, scale = panels[g], pivots_all[g]
            done[g].append(work * jnp.sqrt(scale))
            if step + 1 < order // 8:
                update = dot6(work, work * scale, TN)
                inside = (lane8 >= base) & (lane8 < base + 8)
                for b in range(step + 1, order // 8):
                    blocks[g][b] = jnp.where(inside, 0.0, blocks[g][b]) - update[8 * b:8 * b + 8, :]
    outs = []
    for g in range(count):
        full = jnp.concatenate(done[g], axis=0)
        keep = iota((order, 128), 1) <= iota((order, 128), 0)
        outs.append(jnp.where(keep, full, 0.0))
    return outs


def wide_t(lead, z_t):
    weight = 1.0 / (8.0 * lead.shape[1])
    core_t = weight * dot3(z_t, lead[1])
    return core_t


def diagonal_inverse(far):
    eye = iota(far.shape, 0) == iota(far.shape, 1)
    return 1.0 / jnp.sum(jnp.where(eye, far, 0.0), axis=0, keepdims=True)


def series(pivot, start):
    eye = iota(pivot.shape, 0) == iota(pivot.shape, 1)
    rest = split(jnp.where(eye, 1.0, 0.0) - pivot * start)
    square = split(dot3(rest, rest))
    return rest, square, split(dot3(square, square))


def series_tasks(pivot, start, parts, values=None):
    eye = iota(pivot.shape, 0) == iota(pivot.shape, 1)
    parts.append(split(jnp.where(eye, 1.0, 0.0) - pivot * start))
    half = pivot.shape[0] // 2
    sums = {}

    def block(power, side, left, right):
        at = slice(side * half, side * half + half)
        high = parts[power]
        term = dot1(high[left], high[right][:, at])
        sums[side] = term if (left, right) == (0, 0) else sums[side] + term
        if side and (left, right) == (1, 0):
            parts.append(split(jnp.concatenate([sums[0], sums[1]], axis=1)))

    def apply(power):
        values[0] = values[0] + dot3(values[0], parts[power])

    tasks = []
    for power in range(3):
        if values is not None:
            tasks.append(functools.partial(apply, power))
        if power < 2:
            for side in range(2):
                for pair in ((0, 0), (0, 1), (1, 0)):
                    tasks.append(functools.partial(block, power, side, *pair))
    return tasks


def upper_kernel(flags, far_near, far_u, far_v, corner, out_a, out_b, near, own_u, own_v, sems):
    loads = [
        pltpu.make_async_copy(far_near.at[0], near, sems.at[0]),
        pltpu.make_async_copy(far_u, own_u, sems.at[1]),
        pltpu.make_async_copy(far_v, own_v, sems.at[2]),
    ]
    for load in loads:
        load.start()
    tile, width = own_u.shape[1:]
    weight = 1.0 / (8.0 * tile)
    low_rank = weight * dot3(corner[0], corner[1], NT)
    loads[0].wait()
    far = near[...]
    start = diagonal_inverse(far)
    parts = series(far + low_rank, start)
    for load in loads[1:]:
        load.wait()
    lanes = iota((tile, width), 1)
    values = jnp.concatenate([jnp.where(lanes < flags[2 + s], own_u[s], 0.0).T for s in range(2)], axis=0)
    for part in parts[::-1]:
        values = values + dot3(values, part, NT)
    values = values * start
    out_a[:width] = jnp.where(flags[10] == 0, corner[0].T, values[:width])
    out_a[width:] = own_v[0].T
    out_b[:width] = values[width:]
    out_b[width:] = own_v[1].T


def wide_kernel(flags, lead, crossed, out):
    width = lead.shape[2]
    out[:width] = dot3(wide_t(lead, crossed[:width]), lead[0], NT)
    out[width:] = crossed[width:]


def panel_kernel(order, panel, flags, far_u, far_v, far_near, far_sketch, lead, ours, theirs, *refs):
    if panel == 0:
        corner, extra, to_u, to_v, pack, out_z, out_v = refs[:7]
    else:
        ours_0, theirs_0, to_u, to_v = refs[:4]
    ortho, factor, moved, cu, cv, near, sketch, nu, nv, sems = refs[-10:]
    near_from = far_near.at[1] if panel == 0 else far_near
    loads = [
        pltpu.make_async_copy(far_v, cv, sems.at[0]),
        pltpu.make_async_copy(far_sketch.at[panel], sketch, sems.at[1]),
        pltpu.make_async_copy(far_u, cu, sems.at[2]),
        pltpu.make_async_copy(near_from, near, sems.at[3]),
    ]
    for load in loads:
        load.start()
    tile, width = cu.shape[1:]
    weight = 1.0 / (8.0 * tile)
    root = math.sqrt(tile)
    lanes = iota((tile, width), 1)
    spare = jnp.zeros((width - order, tile), F32)
    row_g = iota((order, width), 0)
    lane_g = iota((order, width), 1)
    eye = (row_g == lane_g).astype(F32)
    even = flags[11] == 0
    full_us, full_vs, bases, grams, units = [], [], [], [], []
    if panel == 1:
        part = ours.shape[1]
        rest = jnp.zeros((width - part, tile), F32)
        lead_u = jnp.concatenate([lead[0], rest], axis=0)
        lead_v = jnp.concatenate([lead[1], rest], axis=0)
    for load in loads:
        load.wait()
    test_t = sketch[...].T[:order]
    for s in range(2):
        own_u = cu[s]
        if panel == 0:
            own_u = jnp.where(lanes < flags[2 + s], own_u, 0.0)
            slot = jnp.where(even, theirs[...], ours[...]) if s == 0 else jnp.where(even, ours[...], theirs[...])
            up_v = slot[width:].T
            side = dot3(lead[0], wide_t(lead, slot[:width]), NT)
        else:
            z_t = jnp.concatenate([jnp.where(even, ours[s], theirs[s]), rest], axis=0)
            up_v = jnp.concatenate([jnp.where(even, theirs[s], ours[s]), rest], axis=0).T
            side = dot3(weight * dot3(z_t, lead_v, NT), lead_u).T
        full_u = jnp.concatenate([own_u, -side], axis=1)
        full_v = jnp.concatenate([cv[s], up_v], axis=1)
        projected = dot3(test_t, full_v)
        basis = dot3(projected, full_u, NT)
        basis = jnp.where(iota((order, tile), 0) < flags[s], basis, 0.0)
        basis = jnp.concatenate([basis, spare], axis=0)
        unit = jnp.where((row_g == lane_g) & (row_g >= flags[s]), 1.0, 0.0)
        grams.append(dot6(basis[:order], basis, NT) + unit)
        full_us.append(full_u)
        full_vs.append(full_v)
        bases.append(basis)
        units.append(unit)

    if panel == 0:
        far = near[...]
        start = diagonal_inverse(far)
        low_rank = dot3(corner[0], corner[1], NT) - dot3(extra[:width], extra[width:], TN)
        parts = []
        tasks = series_tasks(far + weight * low_rank, start, parts)
    else:
        left = flags[10] == 0
        slot = jnp.where(even, theirs_0[...], ours_0[...])
        moved[:part] = jnp.where(even, ours[0], theirs[0])
        moved[part:2 * part] = jnp.where(even, theirs[0], ours[0])
        moved[2 * part:3 * part] = jnp.where(even, ours[2], theirs[2])
        moved[3 * part:] = jnp.where(even, theirs[2], ours[2])
        far = jnp.where(left, near[0], near[1])
        start = diagonal_inverse(far)
        one_u = jnp.where(left, slot[:width], moved[width:2 * width])
        one_v = jnp.where(left, slot[width:], moved[2 * width:])
        two_u = jnp.where(left, 0.0, moved[:width])
        low_rank = dot3(one_u, one_v, TN) - dot3(two_u, slot[width:], TN)
        low = [cv[0].T * start]
        tasks = series_tasks(far + weight * low_rank, start, [], low)

    inverses = eliminate(grams, order, tasks)
    defect = jnp.zeros((), F32)
    for s in range(2):
        once = dot3(inverses[s], bases[s])
        ortho[s, :order] = once
        ortho[s, order:] = spare
        gram = dot3(once, jnp.concatenate([once, spare], axis=0), NT) + units[s]
        factor[s] = gram
        off = gram - eye
        defect = defect + jnp.where(flags[6 + s] == 1, jnp.sum(off * off), 0.0)
    near_unit = defect < 1e-6

    @pl.when(near_unit)
    def _():
        for s in range(2):
            off = factor[s] - eye
            half = jnp.where(lane_g < row_g, off, jnp.where(lane_g == row_g, 0.5 * off, 0.0))
            once = ortho[s]
            ortho[s, :order] = once[:order] - dot1(half.astype(BF16), once.astype(BF16))

    @pl.when(jnp.logical_not(near_unit))
    def _():
        again = eliminate([factor[0], factor[1]], order)
        for s in range(2):
            ortho[s, :order] = dot6(again[s], ortho[s])

    fresh_vs, pending = [], []
    for s in range(2):
        basis = ortho[s]
        back = dot3(basis, full_us[s])
        fresh_v = dot3(full_vs[s], back, NT) * (1.0 / root)
        fresh_u = basis.T * root
        fresh_vs.append(fresh_v)
        keep_u = cu[s]
        keep_v = cv[s]
        if panel == 0:
            keep_u = jnp.where(lanes < flags[2 + s], keep_u, 0.0)
            keep_v = jnp.where(lanes < flags[2 + s], keep_v, 0.0)
        elif s == 0:
            keep_v = jnp.where(flags[8] == 1, low[0].T, keep_v)
            keep_u = jnp.where(flags[9] == 1, 0.0, keep_u)
            keep_v = jnp.where(flags[9] == 1, 0.0, keep_v)
        chosen = flags[6 + s] == 1
        new_u = jnp.where(chosen, fresh_u, keep_u)
        new_v = jnp.where(chosen, fresh_v, keep_v)
        nu[s] = new_u
        nv[s] = new_v
        stores = [
            pltpu.make_async_copy(nu.at[s], to_u.at[s], sems.at[4 + 2 * s]),
            pltpu.make_async_copy(nv.at[s], to_v.at[s], sems.at[5 + 2 * s]),
        ]
        for store in stores:
            store.start()
        pending += stores
    if panel == 0:
        values = jnp.concatenate([ortho[0, :order], ortho[1, :order]], axis=0) * root
        for factors in parts[::-1]:
            values = values + dot3(values, factors, NT)
        values = values * start
        moved[:width] = extra[:width]
        moved[width:2 * width] = corner[0].T
        moved[2 * width:] = corner[1].T
        middle = flags[10] == 1
        fresh_t = fresh_vs[0].T[:order]
        pack[0] = ortho[0, :order] * root
        pack[1] = fresh_t
        out_z[0] = jnp.where(middle, moved[:order], values[:order])
        out_z[1] = values[order:]
        out_z[2] = moved[2 * order:3 * order]
        out_v[0] = jnp.where(middle, moved[order:2 * order], fresh_t)
        out_v[1] = fresh_vs[1].T[:order]
        out_v[2] = moved[3 * order:]
    for store in pending:
        store.wait()


def pack_kernel(flags, own_u, own_v, out, sems):
    loads = [
        pltpu.make_async_copy(own_u.at[0], out.at[0], sems.at[0]),
        pltpu.make_async_copy(own_v.at[0], out.at[1], sems.at[1]),
    ]
    for load in loads:
        load.start()
    for load in loads:
        load.wait()


def call(kernel, shapes, flags, *values, scratch=(), loads=0, stores=0):
    vmem, far = pl.BlockSpec(memory_space=pltpu.VMEM), pl.BlockSpec(memory_space=pltpu.HBM)
    spaces = [pltpu.HBM] * stores + [pltpu.VMEM] * (len(shapes) - stores)
    shapes = tuple(space(shape, F32) for space, shape in zip(spaces, shapes))
    values = [pltpu.with_memory_space_constraint(value, pltpu.HBM) for value in values[:loads]] + list(values[loads:])
    out = pl.pallas_call(
        kernel,
        out_shape=shapes,
        in_specs=[pl.BlockSpec(memory_space=pltpu.SMEM)] + [far] * loads + [vmem] * (len(values) - loads),
        out_specs=(far,) * stores + (vmem,) * (len(shapes) - stores),
        scratch_shapes=list(scratch),
        compiler_params=pltpu.CompilerParams(vmem_limit_bytes=24 * 1024 * 1024),
    )(flags, *values)
    return out if len(out) > 1 else out[0]


Z_COUNT = 4
X_COUNT = 4
COLS = 4


def row_of(z, x, core):
    return (z * X_COUNT + x) * 2 + core


def fan_out(value, axis, pair_sets):
    total = None
    for pairs in pair_sets:
        moved = lax.ppermute(value, axis, pairs)
        total = moved if total is None else total + moved
    return total


def share_planes(mine, row, before, beside):
    core = row % 2
    x = (row // 2) % X_COUNT
    z = row // (2 * X_COUNT)
    first = fan_out(
        mine,
        "row",
        [[(row_of(0, 0, 0), row_of(k, 0, 0)), (row_of(0, 0, 1), row_of(0, k, 1))] for k in (1, 3, 2)],
    )
    held, before = lax.optimization_barrier((jnp.where(row < 2, mine, first), before))
    second = fan_out(
        held,
        "row",
        [
            [(row_of(z, 0, 0), row_of(z, k, 0)) for z in range(Z_COUNT)]
            + [(row_of(0, x, 1), row_of(k, x, 1)) for x in range(X_COUNT)]
            for k in (1, 3, 2)
        ],
    )
    holder = jnp.where(core == 0, x, z) == 0
    final, beside = lax.optimization_barrier((jnp.where(holder, held, second), beside))
    other = lax.ppermute(final, "row", [(r, r ^ 1) for r in range(2 * X_COUNT * Z_COUNT)])
    return final, other, before, beside


def share_row(value, root, col, lowest):
    right, left, far = (root + 1) % COLS, (root + 3) % COLS, (root + 2) % COLS
    count = 2 * X_COUNT * Z_COUNT

    def pairs_of(pairs):
        return [(r * COLS + a, r * COLS + b) for r in range(lowest, count) for a, b in pairs]

    one = lax.ppermute(value, ("row", "col"), pairs_of([(root, right)]))
    held = jnp.where(col == root, value, one)

    def finish(held):
        two = lax.ppermute(held, ("row", "col"), pairs_of([(root, left), (right, far)]))
        return jnp.where((col == root) | (col == right), held, two)

    return held, finish


def share_pivots(value, roots):
    shares = [
        lax.ppermute(value, ("row", "col"), [(r * COLS + c, r * COLS + (c + k) % COLS) for r, c in roots])
        for k in (1, 3, 2)
    ]
    return shares[0], shares[1] + shares[2]


def body(factor_u, factor_v, near_field, sketch, tile_ranks):
    tile, width = factor_u.shape[4:]
    row = lax.axis_index("row")
    col = lax.axis_index("col")
    core = row % 2
    own_u = factor_u.reshape(2, tile, width)
    own_v = factor_v.reshape(2, tile, width)
    ranks = tile_ranks.reshape(3, -1, 2)
    own_ranks = lax.dynamic_slice_in_dim(ranks, row, 1, 1)[:, 0]
    order = (width - width // 4, width - width // 4 - (width - width // 4) // 4)

    def flags_of(panel):
        slots = jnp.arange(2) * 4 + col
        chosen = (row > panel) & (slots > panel)
        if panel == 0:
            chosen = chosen & jnp.logical_not((row == 1) & (slots == 1))
        lower = (row > col) & (col < 2)
        pivot = (row == col) & (col < 2)
        parts = [own_ranks[panel + 1], own_ranks[0], ranks[0, 0], chosen]
        parts += [lower[None], pivot[None], col[None], core[None]]
        return jnp.concatenate([part.astype(jnp.int32) for part in parts])

    flags = [flags_of(panel) for panel in range(2)]
    pair, payload = (2, tile, width), (2 * width, tile)
    packed = (3, order[0], tile)
    scratch = [
        [pltpu.VMEM((2, width, tile), F32), pltpu.VMEM((2, order[k], width), F32), pltpu.VMEM((4 * order[0], tile), F32)]
        + [pltpu.VMEM(shape, F32) for shape in (pair, pair, ((tile, tile), (2, tile, tile))[k], (tile, width), pair, pair)]
        + [pltpu.SemaphoreType.DMA((8,))]
        for k in range(2)
    ]

    with jax.named_scope("corner_share"):
        pack = call(
            pack_kernel, (pair,), col[None].astype(jnp.int32), own_u, own_v,
            scratch=[pltpu.SemaphoreType.DMA((2,))], loads=2,
        )
        near, others = share_pivots(pack, [(0, 0), (1, 1)])
        keep = jnp.arange(width, dtype=jnp.int32) < own_ranks[0, 0]
        kept, near = lax.optimization_barrier((pack, near))
        near_lead, finish = share_row(jnp.where(keep, kept, 0.0), 0, col, 1)
        got = near + others
        corner = jnp.where(col == row, pack, got)
    with jax.named_scope("first_upper"):
        up_a, up_b = call(
            upper_kernel, (payload, payload), flags[0], near_field, own_u, own_v, corner,
            scratch=[pltpu.VMEM(shape, F32) for shape in ((tile, tile), pair, pair)] + [pltpu.SemaphoreType.DMA((3,))],
            loads=3,
        )
    with jax.named_scope("upper_share"):
        crossed = lax.ppermute(up_a, "row", [(0, 1)])
        extra = call(wide_kernel, (payload,), flags[0], near_lead, crossed)
        mine, extra = lax.optimization_barrier((jnp.where(core == 0, up_b, crossed), extra))
        got = sum(share_pivots(extra, [(1, 1)]))
        ours_0, theirs_0, near_lead, got = share_planes(mine, row, near_lead, got)
        lead = finish(near_lead)
        extra = jnp.where(col == row, extra, got)
    with jax.named_scope("first_update"):
        cur_u, cur_v, pack, out_z, out_v = call(
            functools.partial(panel_kernel, order[0], 0),
            (pair, pair, (2, order[0], tile), packed, packed),
            flags[0], own_u, own_v, near_field, sketch, lead, ours_0, theirs_0, corner, extra,
            scratch=scratch[0], loads=4, stores=2,
        )
    with jax.named_scope("second_share"):
        near_lead, finish = share_row(pack, 1, col, 0)
        crossed = lax.ppermute(out_z, "row", [(1, 0)])
        ours, theirs, near_lead, _ = share_planes(jnp.where(core == 1, out_v, crossed), row, near_lead, row)
        lead = finish(near_lead)
    with jax.named_scope("second_update"):
        cur_u, cur_v = call(
            functools.partial(panel_kernel, order[1], 1),
            (pair, pair),
            flags[1], cur_u, cur_v, near_field, sketch, lead, ours, theirs, ours_0, theirs_0,
            scratch=scratch[1], loads=4, stores=2,
        )
    shape_out = factor_u.shape
    return cur_u.reshape(shape_out), cur_v.reshape(shape_out)


def solution(mesh):
    tiles = P(None, "row", None, "col", None, None)
    return jax.shard_map(
        body,
        mesh=mesh,
        in_specs=(tiles, tiles, P(), P(), P(None, None, None, None, "col")),
        out_specs=(tiles, tiles),
        check_vma=False,
    )
```
